128 devices in a mesh: rows: 8 (over z, core), tensor: 16 (over y, x).
Axes of the slice: x: 4, y: 4, z: 4, core: 2. Of those that a mesh axis runs over, the one named last changes fastest.
Arguments:
- base_hidden: bfloat16 [512, 8192], P('rows', 'tensor'), may hold values from -360 to 360
- expert_hidden: bfloat16 [512, 4096], P('rows', 'tensor'), may hold values from -360 to 360
- anti_hidden: bfloat16 [512, 4096], P('rows', 'tensor'), may hold values from -360 to 360
- base_gain: bfloat16 [8192], P('tensor'), may hold values from 0.5 to 1.5
- expert_gain: bfloat16 [4096], P('tensor'), may hold values from 0.5 to 1.5
- anti_gain: bfloat16 [4096], P('tensor'), may hold values from 0.5 to 1.5
- base_head: bfloat16 [8192, 16, 4096], P('tensor', None, 'rows'), may hold values from -60 to 60
- expert_head: bfloat16 [4096, 16, 4096], P('tensor', None, 'rows'), may hold values from -0.09375 to 0.09375
- anti_head: bfloat16 [4096, 16, 4096], P('tensor', None, 'rows'), may hold values from -0.09375 to 0.09375
- strength: float32 [1], replicated, may hold values from 0.5 to 2
- token_ids: int32 [512], P('rows'), may hold values from 0 to 65535
Outputs:
- log_probs: float32 [512, 65536], P('rows', 'tensor')
- picked: float32 [512], P('rows')
The draws below stay inside these ranges and needn't reach their ends.
All inputs are finite; a program needn't handle non-finite values.
Results may differ from the reference program's by a relative error of at most 0.0022.
Values may be sent and summed in bfloat16 or wider, within the bound.
No kernel may reach another device: no remote copies, remote signals or barrier semaphores. Data moves between devices by JAX's collectives and lax.ppermute only.
A program may use at most 384 MiB of HBM per device.

```python
import math
import jax
import jax.numpy as jnp
from jax import lax

D = 8192
DE = 4096
VOCAB = 65536
TOKENS = 512
N_TENSOR = 16


def rough_hidden(key, salt, width):
    inner = jax.random.fold_in(key, salt)
    first, second, third = jax.random.split(inner, 3)
    noise = jnp.clip(jax.random.normal(first, (TOKENS, width), jnp.float32), -4.0, 4.0)
    row_scale = jnp.exp(jax.random.uniform(second, (TOKENS, 1), jnp.float32) * math.log(10.0))
    rising = jnp.exp(jnp.arange(width, dtype=jnp.float32) / width * math.log(3.0))
    col_scale = jnp.exp(jax.random.uniform(third, (1, width), jnp.float32) * math.log(10.0)) * rising[None, :]
    values = noise * row_scale * col_scale / 10.0
    return values


def draw_base_hidden(key, part):
    values = rough_hidden(key, 11, D)
    return values.astype(jnp.bfloat16)


def draw_expert_hidden(key, part):
    return rough_hidden(key, 23, DE).astype(jnp.bfloat16)


def draw_anti_hidden(key, part):
    return rough_hidden(key, 37, DE).astype(jnp.bfloat16)


def draw_base_head(key, part):
    inner = jax.random.fold_in(key, 51)
    first, second = jax.random.split(inner, 2)
    noise = jnp.clip(jax.random.normal(first, (D, VOCAB), jnp.float32), -4.0, 4.0)
    rising = jnp.exp(jnp.arange(VOCAB, dtype=jnp.float32) / VOCAB * math.log(3.0))
    col_scale = 0.3 * jnp.exp(jax.random.uniform(second, (VOCAB,), jnp.float32) * math.log(10.0)) * rising
    values = noise * col_scale[None, :] / math.sqrt(D)
    return values.reshape(D, N_TENSOR, VOCAB // N_TENSOR).astype(jnp.bfloat16)


def plant(values, own_key, smallest, high):
    spot = [jax.random.randint(jax.random.fold_in(own_key, axis), (), 0, length) for axis, length in enumerate(values.shape)]
    widest = values.shape.index(max(values.shape))
    next_to = spot[:widest] + [(spot[widest] + 1) % values.shape[widest]] + spot[widest + 1:]
    return values.at[tuple(spot)].set(smallest).at[tuple(next_to)].set(high)


def block_levels(own_key, extent, cuts, smallest, top_value):
    def one(dim, shards_of):
        steps = jax.random.uniform(jax.random.fold_in(jax.random.fold_in(own_key, 6), dim), (shards_of,), jnp.float32, smallest / len(cuts), top_value / len(cuts))
        return jnp.repeat(jnp.exp(steps), extent[dim] // shards_of).reshape((-1,) + (1,) * (len(extent) - dim - 1))

    factor_of = one(*cuts[0])
    for cut in cuts[1:]:
        factor_of = factor_of * one(*cut)
    return factor_of


def normal_values(stream_key, shape, deviation, reach, pieces=(), held_as=jnp.bfloat16):
    loudness = block_levels(stream_key, shape, pieces, -0.22, 0.18) if pieces else 1.0
    result = jax.random.normal(stream_key, shape, jnp.float32) * deviation * loudness
    return jnp.minimum(jnp.maximum(result, -reach), reach).astype(held_as)


def setup_inputs(seed: int = 0) -> dict:
    seeds = jax.random.split(jax.random.key(seed), 12)
    return {
        "base_hidden": draw_base_hidden(jax.random.fold_in(seeds[11], 71), 0),
        "expert_hidden": draw_expert_hidden(jax.random.fold_in(seeds[11], 71), 0),
        "anti_hidden": draw_anti_hidden(jax.random.fold_in(seeds[11], 71), 0),
        "base_gain": jnp.clip(1.0 + 0.1 * jax.random.normal(seeds[3], (D,), jnp.float32), 0.5, 1.5).astype(jnp.bfloat16),
        "expert_gain": jnp.clip(1.0 + 0.1 * jax.random.normal(seeds[4], (DE,), jnp.float32), 0.5, 1.5).astype(jnp.bfloat16),
        "anti_gain": jnp.clip(1.0 + 0.1 * jax.random.normal(seeds[5], (DE,), jnp.float32), 0.5, 1.5).astype(jnp.bfloat16),
        "base_head": draw_base_head(jax.random.fold_in(seeds[11], 71), 0),
        "expert_head": normal_values(seeds[7], (DE, N_TENSOR, VOCAB // N_TENSOR), DE ** -0.5, 0.09375, ((0, 16), (2, 8))),
        "anti_head": normal_values(seeds[8], (DE, N_TENSOR, VOCAB // N_TENSOR), DE ** -0.5, 0.09375, ((0, 16), (2, 8))),
        "strength": jnp.clip(jax.random.uniform(seeds[9], (1,), jnp.float32, 0.5, 2.0), 0.5, 2.0),
        "token_ids": plant(jax.random.randint(seeds[10], (TOKENS,), 0, VOCAB), jax.random.fold_in(seeds[10], 1), 0, VOCAB - 1).astype(jnp.int32),
    }


def normalize(hidden, gain):
    values = hidden.astype(jnp.float32)
    meansq = lax.optimization_barrier(jnp.mean(values * values, axis=1, keepdims=True))
    return (values * lax.rsqrt(meansq + 1e-05) * gain.astype(jnp.float32)).astype(jnp.bfloat16)

def head_logits(normed, head):
    values = normed.astype(jnp.float32)

    def block(weights):
        return jnp.dot(values, weights.astype(jnp.float32), precision=lax.Precision.HIGHEST)
    blocks = lax.map(block, jnp.moveaxis(head, 1, 0))
    return jnp.moveaxis(blocks, 0, 1).reshape(values.shape[0], -1)

def reference(base_hidden, expert_hidden, anti_hidden, base_gain, expert_gain, anti_gain, base_head, expert_head, anti_head, strength, token_ids):
    normed_base = normalize(base_hidden, base_gain)
    normed_expert = normalize(expert_hidden, expert_gain)
    normed_anti = normalize(anti_hidden, anti_gain)
    base_logits = head_logits(normed_base, base_head)
    expert_logits = head_logits(normed_expert, expert_head)
    anti_logits = head_logits(normed_anti, anti_head)
    combined = base_logits + strength[0] * (expert_logits - anti_logits)
    largest = lax.optimization_barrier(jnp.max(combined, axis=1, keepdims=True))
    logz = largest + jnp.log(lax.optimization_barrier(jnp.sum(jnp.exp(combined - largest), axis=1, keepdims=True)))
    log_probs = combined - logz
    picked = jnp.take_along_axis(log_probs, token_ids[:, None].astype(jnp.int32), axis=1)[:, 0]
    return (log_probs, picked)
```

```python
import jax
import jax.numpy as jnp
import numpy as np
from jax import lax
from jax.experimental import pallas as pl
from jax.experimental.pallas import tpu as pltpu
from jax.sharding import PartitionSpec as P

D = 8192
DE = 4096
NZ, NC, NY, NX = 4, 2, 4, 4
AXES = ("rows", "tensor")
BF = jnp.bfloat16
F16 = jnp.float16
F32 = jnp.float32
DOWN, UP = 0.0625, 16.0


def device(z, c, y, x):
    return (z * NC + c) * (NY * NX) + y * NX + x


def exchange(value, axis, stage):
    pairs = []
    for z in range(NZ):
        for c in range(NC):
            u = 1 if (stage + c) % 2 == 0 else 3
            for y in range(NY):
                for x in range(NX):
                    to = {
                        "z": (z ^ u, c, y, x),
                        "y": (z, c, y ^ u, x),
                        "x": (z, c, y, x ^ u),
                        "core": (z, 1 - c, y, x),
                    }[axis]
                    pairs.append((device(z, c, y, x), device(*to)))
    return lax.ppermute(value, AXES, pairs)


def tables():
    out = np.zeros((NZ * NC * NY * NX, 48), np.int32)
    for z in range(NZ):
        for c in range(NC):
            u, v = (1, 3) if c == 0 else (3, 1)
            first, second = (2, u, v, 0), (u, 2, 0, v)
            for y in range(NY):
                for x in range(NX):
                    row = [(y ^ j) * NX + (x ^ i) for i in first for j in second]
                    row += [(y ^ i) * NX + (x ^ j) for i in first for j in second]
                    row += [(z ^ i) * NC + k for i in (0, u, v, 2) for k in (c, 1 - c)]
                    out[device(z, c, y, x), : len(row)] = row
    return out


def relay_kernel(head, out):
    out[...] = jnp.swapaxes(head[...], 0, 1)


def relay(head, start, count, step=64):
    _, n_a, c = head.shape
    out = pl.pallas_call(
        relay_kernel,
        grid=(count // step,),
        in_specs=[pl.BlockSpec((step, n_a, c), lambda i: (start // step + i, 0, 0))],
        out_specs=pl.BlockSpec((n_a, step, c), lambda i: (0, i, 0)),
        out_shape=jax.ShapeDtypeStruct((n_a, count, c), head.dtype),
        cost_estimate=pl.CostEstimate(flops=10**10, bytes_accessed=2**24, transcendentals=0),
    )(head)
    return pltpu.with_memory_space_constraint(out, pltpu.HBM)


def matmul_kernel(table, alpha, *refs):
    xs, ws, out = refs[:8], refs[8:12], refs[12]
    tokens = xs[0].shape[0]
    for i in range(2):
        base0, base1, expert, anti = [
            jnp.dot(x[...], w[0], preferred_element_type=F32) for x, w in zip(xs[i::2], ws)
        ]
        total = base0 + base1 + alpha[0] * (expert - anti)
        out[0, i * tokens : (i + 1) * tokens] = total.astype(out.dtype)


def project(table, alpha, acts, heads, first, half, dtype):
    tokens = acts[0].shape[0]
    half_c = heads[0].shape[2] // 2
    quarter = heads[0].shape[1]

    def features(i):
        return pl.BlockSpec((tokens, quarter), lambda _, tab: (0, i))

    def weights():
        return pl.BlockSpec((1, quarter, half_c), lambda i, tab: (tab[first + i], 0, half))

    return pl.pallas_call(
        matmul_kernel,
        grid_spec=pltpu.PrefetchScalarGridSpec(
            num_scalar_prefetch=1,
            grid=(4,),
            in_specs=[pl.BlockSpec(memory_space=pltpu.SMEM)]
            + [features(i) for i in range(4) for _ in acts]
            + [weights() for _ in heads],
            out_specs=pl.BlockSpec((1, 2 * tokens, half_c), lambda i, tab: (i, 0, 0)),
        ),
        out_shape=jax.ShapeDtypeStruct((4, 2 * tokens, half_c), dtype),
        compiler_params=pltpu.CompilerParams(vmem_limit_bytes=32 << 20),
        cost_estimate=pl.CostEstimate(flops=1, bytes_accessed=1, transcendentals=0),
    )(table, alpha, *acts * 4, *heads)


def wide(value):
    return value.astype(F32) * UP if value.dtype == F16 else value.astype(F32)


def narrow(value):
    return (value * DOWN).astype(F16)


def together(*values):
    return lax.optimization_barrier(values)


def merge(stats):
    top = jnp.max(stats[:, 0], axis=0)
    total = jnp.sum(stats[:, 1] * jnp.exp(stats[:, 0] - top[None]), axis=0)
    return top + jnp.log(total), jnp.sum(stats[:, 2], axis=0)


def final_kernel(source, logits, logz, out):
    width = logits.shape[2]
    for i in range(logits.shape[0]):
        at = pl.multiple_of(source[i] * width, width)
        out[:, pl.ds(at, width)] = logits[i] - logz[...]


def shards(
    base_hidden,
    expert_hidden,
    anti_hidden,
    base_gain,
    expert_gain,
    anti_gain,
    base_head,
    expert_head,
    anti_head,
    strength,
    token_ids,
):
    r = lax.axis_index("rows")
    t = lax.axis_index("tensor")
    rows, c_width = token_ids.shape[0], base_head.shape[2]
    mine = lax.dynamic_slice(jnp.asarray(tables()), (r * (NY * NX) + t, 0), (1, 48))[0]
    table, source = mine[:32], mine[32:40]

    values = [h.astype(F32) for h in (base_hidden, expert_hidden, anti_hidden)]
    sq = jnp.stack([jnp.sum(h * h, axis=1) for h in values])
    quarter = expert_head.shape[0]
    raw = ((base_head, 0), (base_head, quarter), (expert_head, 0), (anti_head, 0))
    heads = []
    for i, (axis, stage) in enumerate((("x", 0), ("x", 1), ("y", 0), ("y", 1))):
        head, start = raw[i]
        sq, head = together(sq, head)
        got, head = together(exchange(sq, axis, stage), relay(head, start, quarter))
        heads.append(head)
        sq = sq + got
    widths = (D, DE, DE)
    gains = (base_gain, expert_gain, anti_gain)
    normed = jnp.concatenate(
        [
            h * lax.rsqrt(sq[i] / widths[i] + 1e-05)[:, None] * gains[i].astype(F32)
            for i, h in enumerate(values)
        ],
        axis=1,
    ).astype(BF)

    pair = exchange(normed, "z", 0)
    far = exchange(jnp.stack([normed, pair]), "z", 1)
    mine = jnp.concatenate([pair, far[1], normed, far[0]])
    acts = [mine, exchange(mine, "core", 0)]

    axes = (("x", "y"), ("y", "x"))
    kept = [[], []]
    moved = [[], []]
    for i in range(4):
        for half in range(2):
            part = project(table, strength, acts, heads, 16 * half + 4 * i, half, BF if i < 2 else F32)
            table, part = together(table, part)
            if i < 2:
                moved[half].append(exchange(part, axes[half][0], 0))
            else:
                kept[half].append(part)
    second_step = [
        exchange(narrow(kept[h][0] + wide(moved[h][0])), axes[h][0], 1) for h in range(2)
    ]
    sums = [kept[h][1] + wide(moved[h][1]) + wide(second_step[h]) for h in range(2)]
    moved = [exchange(narrow(sums[h][:2]), axes[h][1], 0) for h in range(2)]
    second_step = [
        exchange(narrow(sums[h][3] + wide(moved[h][1])), axes[h][1], 1) for h in range(2)
    ]
    logits = jnp.concatenate(
        [narrow(sums[h][2] + wide(moved[h][0]) + wide(second_step[h])) for h in range(2)], axis=1
    ).reshape(NC, NZ, rows, c_width)

    other = exchange(logits[1], "core", 0)
    both = jnp.stack([logits[0], other], axis=1)
    near = exchange(both[:2], "z", 0)
    last = exchange(jnp.stack([both[3], near[1]]), "z", 1)
    home = jnp.concatenate([both[2], near[0], last[0], last[1]]).astype(F32) * UP
    top = jnp.max(home, axis=(0, 2))
    total = jnp.sum(jnp.exp(home - top[None, :, None]), axis=(0, 2))
    column = source[:, None, None] * c_width + lax.broadcasted_iota(jnp.int32, (8, 1, c_width), 2)
    wanted = (token_ids - t * (8 * c_width))[None, :, None]
    pick = jnp.sum(jnp.where(column == wanted, home, 0.0), axis=(0, 2))
    stats = jnp.stack([top, total, pick])
    stats = lax.all_to_all(
        jnp.broadcast_to(stats[None], (NY * NX, 3, rows)), "tensor", 0, 0, tiled=True
    )
    logz, pick = merge(stats)

    log_probs = pl.pallas_call(
        final_kernel,
        in_specs=[
            pl.BlockSpec(memory_space=pltpu.SMEM),
            pl.BlockSpec(memory_space=pltpu.VMEM),
            pl.BlockSpec(memory_space=pltpu.VMEM),
        ],
        out_specs=pl.BlockSpec(memory_space=pltpu.VMEM),
        out_shape=jax.ShapeDtypeStruct((rows, 8 * c_width), F32),
    )(source, home, logz[:, None])
    return log_probs, pick - logz


def solution(mesh):
    return jax.shard_map(
        shards,
        mesh=mesh,
        in_specs=(
            P("rows", "tensor"),
            P("rows", "tensor"),
            P("rows", "tensor"),
            P("tensor"),
            P("tensor"),
            P("tensor"),
            P("tensor", None, "rows"),
            P("tensor", None, "rows"),
            P("tensor", None, "rows"),
            P(),
            P("rows"),
        ),
        out_specs=(P("rows", "tensor"), P("rows")),
        check_vma=False,
    )
```

```python
import functools

import jax
import jax.numpy as jnp
import numpy as np
from jax import lax
from jax.experimental import pallas as pl
from jax.experimental.pallas import tpu as pltpu
from jax.sharding import PartitionSpec as P

D = 8192
DE = 4096
NZ, NC, NY, NX = 4, 2, 4, 4
AXES = ("rows", "tensor")
BF = jnp.bfloat16
F16 = jnp.float16
F32 = jnp.float32
DOWN, UP = 0.0625, 16.0


def device(z, c, y, x):
    return (z * NC + c) * (NY * NX) + y * NX + x


def exchange(value, axis, stage):
    pairs = []
    for z in range(NZ):
        for c in range(NC):
            u = 1 if (stage + c) % 2 == 0 else 3
            for y in range(NY):
                for x in range(NX):
                    to = {
                        "z": (z ^ u, c, y, x),
                        "y": (z, c, y ^ u, x),
                        "x": (z, c, y, x ^ u),
                        "core": (z, 1 - c, y, x),
                    }[axis]
                    pairs.append((device(z, c, y, x), device(*to)))
    return lax.ppermute(value, AXES, pairs)


def tables():
    out = np.zeros((NZ * NC * NY * NX, 48), np.int32)
    for z in range(NZ):
        for c in range(NC):
            u, v = (1, 3) if c == 0 else (3, 1)
            first, second = (2, u, v, 0), (u, 2, 0, v)
            for y in range(NY):
                for x in range(NX):
                    row = [(y ^ j) * NX + (x ^ i) for i in first for j in second]
                    row += [(y ^ i) * NX + (x ^ j) for i in first for j in second]
                    row += [(z ^ i) * NC + k for i in (0, u, v, 2) for k in (c, 1 - c)]
                    out[device(z, c, y, x), : len(row)] = row
    return out


def relay_kernel(head, out):
    out[...] = jnp.swapaxes(head[...], 0, 1)


def relay(head, start, count, step=64):
    _, n_a, c = head.shape
    return pl.pallas_call(
        relay_kernel,
        grid=(count // step,),
        in_specs=[pl.BlockSpec((step, n_a, c), lambda i: (start // step + i, 0, 0))],
        out_specs=pl.BlockSpec((n_a, step, c), lambda i: (0, i, 0)),
        out_shape=jax.ShapeDtypeStruct((n_a, count, c), head.dtype),
        compiler_params=pltpu.CompilerParams(vmem_limit_bytes=12 << 20),
        cost_estimate=pl.CostEstimate(flops=10**10, bytes_accessed=2**24, transcendentals=0),
    )(head)


def matmul_kernel(table, alpha, xb0, xb1, xe, xa, wb0, wb1, we, wa, out):
    base0, base1, expert, anti = [
        jnp.dot(x[...], w[0], preferred_element_type=F32)
        for x, w in ((xb0, wb0), (xb1, wb1), (xe, we), (xa, wa))
    ]
    out[0] = (base0 + base1 + alpha[0] * (expert - anti)).astype(out.dtype)


def project(table, alpha, acts, heads, first, half, dtype):
    tokens = acts.shape[0]
    half_c = heads[0].shape[2] // 2
    quarter = heads[0].shape[1]

    def features(i):
        return pl.BlockSpec((tokens, quarter), lambda _, tab: (0, i))

    def weights():
        return pl.BlockSpec((1, quarter, half_c), lambda i, tab: (tab[first + i], 0, half))

    return pl.pallas_call(
        matmul_kernel,
        grid_spec=pltpu.PrefetchScalarGridSpec(
            num_scalar_prefetch=1,
            grid=(4,),
            in_specs=[pl.BlockSpec(memory_space=pltpu.SMEM)]
            + [features(i) for i in range(4)]
            + [weights() for _ in heads],
            out_specs=pl.BlockSpec((1, tokens, half_c), lambda i, tab: (i, 0, 0)),
        ),
        out_shape=jax.ShapeDtypeStruct((4, tokens, half_c), dtype),
        compiler_params=pltpu.CompilerParams(vmem_limit_bytes=12 << 20),
        cost_estimate=pl.CostEstimate(flops=1, bytes_accessed=1, transcendentals=0),
    )(table, alpha, *[acts] * 4, *heads)


def wide(value):
    return value.astype(F32) * UP if value.dtype == F16 else value.astype(F32)


def narrow(value):
    return (value * DOWN).astype(F16)


def in_hbm(value):
    return pltpu.with_memory_space_constraint(value, pltpu.HBM)


def together(*values):
    return lax.optimization_barrier(values)


def lanes(columns, rows):
    lane = lax.broadcasted_iota(jnp.int32, (rows, 128), 1)
    out = jnp.zeros((rows, 128), F32)
    for i, column in enumerate(columns):
        out = jnp.where(lane == i, column, out)
    return out


def square_kernel(*refs):
    values = [h[...].astype(F32) for h in refs[:-1]]
    sums = [jnp.sum(h * h, axis=1, keepdims=True) for h in values]
    refs[-1][...] = lanes(sums, refs[-1].shape[0])


def norm_kernel(widths, *refs):
    hidden, gains, sq, got, out = refs[:3], refs[3:6], refs[6], refs[7], refs[8]
    total = sq[...] + got[...]
    at = 0
    for i, h in enumerate(hidden):
        scale = lax.rsqrt(total[:, i : i + 1] / widths[i] + 1e-05)
        value = h[...].astype(F32) * scale * gains[i][...].astype(F32)
        out[:, at : at + h.shape[1]] = value.astype(out.dtype)
        at += h.shape[1]


def stats_kernel(source, home, wanted, out):
    pieces, rows, width = home.shape
    top = jnp.max(home[...], axis=(0,))
    top = jnp.max(top, axis=1, keepdims=True)
    total = jnp.zeros((rows, width), F32)
    pick = jnp.zeros((rows, width), F32)
    lane = lax.broadcasted_iota(jnp.int32, (rows, width), 1)
    for i in range(pieces):
        value = home[i]
        total += jnp.exp(value - top)
        pick += jnp.where(lane == wanted[...] - source[i] * width, value, 0.0)
    total = jnp.sum(total, axis=1, keepdims=True)
    pick = jnp.sum(pick, axis=1, keepdims=True)
    square = jnp.concatenate([lanes([top, total, pick], rows), jnp.zeros((128 - rows, 128), F32)])
    out[...] = jnp.broadcast_to(square.T[None, :8], out.shape)


def final_kernel(source, home, stats, out, picked):
    pieces, rows, width = home.shape
    tops, totals, picks = [stats[:, i, :rows] for i in range(3)]
    top = jnp.max(tops, axis=0, keepdims=True)
    logz = top + jnp.log(jnp.sum(totals * jnp.exp(tops - top), axis=0, keepdims=True))
    picked[...] = jnp.sum(picks, axis=0, keepdims=True) - logz
    square = jnp.concatenate(
        [jnp.broadcast_to(logz, (128, rows)), jnp.zeros((128, 128 - rows), F32)], axis=1
    )
    column = square.T[:rows, :1]
    for i in range(pieces):
        at = pl.multiple_of(source[i] * width, width)
        out[:, pl.ds(at, width)] = home[i] - column


def call(kernel, shapes, *args):
    def spec(v):
        small = v.ndim == 1 and v.dtype == jnp.int32
        return pl.BlockSpec(memory_space=pltpu.SMEM) if small else pl.BlockSpec()

    outs = [jax.ShapeDtypeStruct(s, d) for s, d in shapes]
    result = pl.pallas_call(
        kernel,
        in_specs=[spec(v) for v in args],
        out_specs=[pl.BlockSpec() for _ in outs],
        out_shape=outs,
        compiler_params=pltpu.CompilerParams(vmem_limit_bytes=16 << 20),
    )(*args)
    return result if len(outs) > 1 else result[0]


def shards(
    base_hidden,
    expert_hidden,
    anti_hidden,
    base_gain,
    expert_gain,
    anti_gain,
    base_head,
    expert_head,
    anti_head,
    strength,
    token_ids,
):
    r = lax.axis_index("rows")
    t = lax.axis_index("tensor")
    rows, c_width = token_ids.shape[0], base_head.shape[2]
    mine = lax.dynamic_slice(jnp.asarray(tables()), (r * (NY * NX) + t, 0), (1, 48))[0]
    table, source = mine[:32], mine[32:40]

    quarter = expert_head.shape[0]
    base = in_hbm(base_head)
    raw = [(base, 0), (base, quarter), (expert_head, 0), (anti_head, 0)]
    heads = []

    def swap(value, axis, stage, beside):
        if not beside:
            return exchange(value, axis, stage)
        head, start = raw[len(heads)]
        value, head = together(value, head)
        got, head = together(exchange(value, axis, stage), relay(head, start, quarter))
        heads.append(head)
        return got

    hidden = (base_hidden, expert_hidden, anti_hidden)
    gains = [g[None] for g in (base_gain, expert_gain, anti_gain)]
    sq = call(square_kernel, [((rows, 128), F32)], *[in_hbm(h) for h in hidden])
    sq += swap(sq, "x", 0, False)
    sq += swap(sq, "x", 1, True)
    sq += swap(sq, "y", 0, False)
    got = swap(sq, "y", 1, True)
    width = sum(h.shape[1] for h in hidden)
    normed = call(
        functools.partial(norm_kernel, (D, DE, DE)), [((rows, width), BF)], *hidden, *gains, sq, got
    )
    pair = swap(normed, "z", 0, True)
    far = swap(jnp.stack([normed, pair]), "z", 1, True)
    mine = jnp.concatenate([pair, far[1], normed, far[0]])
    acts = jnp.concatenate([mine, exchange(mine, "core", 0)])

    axes = (("x", "y"), ("y", "x"))
    kept = [[], []]
    moved = [[], []]
    for i in range(4):
        for half in range(2):
            part = project(table, strength, acts, heads, 16 * half + 4 * i, half, BF if i < 2 else F32)
            table, part = together(table, part)
            if i < 2:
                moved[half].append(exchange(part, axes[half][0], 0))
            else:
                kept[half].append(part)
    second_step = [
        exchange(narrow(kept[h][0] + wide(moved[h][0])), axes[h][0], 1) for h in range(2)
    ]
    sums = [kept[h][1] + wide(moved[h][1]) + wide(second_step[h]) for h in range(2)]
    moved = [exchange(narrow(sums[h][:2]), axes[h][1], 0) for h in range(2)]
    second_step = [
        exchange(narrow(sums[h][3] + wide(moved[h][1])), axes[h][1], 1) for h in range(2)
    ]
    logits = jnp.concatenate(
        [narrow(sums[h][2] + wide(moved[h][0]) + wide(second_step[h])) for h in range(2)], axis=1
    ).reshape(NC, NZ, rows, c_width)

    other = exchange(logits[1], "core", 0)
    both = jnp.stack([logits[0], other], axis=1)
    near = exchange(both[:2], "z", 0)
    last = exchange(jnp.stack([both[3], near[1]]), "z", 1)
    home = jnp.concatenate([both[2], near[0], last[0], last[1]]).astype(F32) * UP
    wanted = (token_ids - t * (8 * c_width))[:, None]
    stats = call(stats_kernel, [((NY * NX, 8, 128), F32)], source, home, wanted)
    stats = lax.all_to_all(stats, "tensor", 0, 0, tiled=True)
    log_probs, picked = call(
        final_kernel, [((rows, 8 * c_width), F32), ((1, rows), F32)], source, home, stats
    )
    return log_probs, picked[0]


def solution(mesh):
    return jax.shard_map(
        shards,
        mesh=mesh,
        in_specs=(
            P("rows", "tensor"),
            P("rows", "tensor"),
            P("rows", "tensor"),
            P("tensor"),
            P("tensor"),
            P("tensor"),
            P("tensor", None, "rows"),
            P("tensor", None, "rows"),
            P("tensor", None, "rows"),
            P(),
            P("rows"),
        ),
        out_specs=(P("rows", "tensor"), P("rows")),
        check_vma=False,
    )
```

```python
import functools

import jax
import jax.numpy as jnp
import numpy as np
from jax import lax
from jax.experimental import pallas as pl
from jax.experimental.pallas import tpu as pltpu
from jax.sharding import PartitionSpec as P

D = 8192
DE = 4096
NZ, NC, NY, NX = 4, 2, 4, 4
AXES = ("rows", "tensor")
BF = jnp.bfloat16
F16 = jnp.float16
F32 = jnp.float32
DOWN, UP = 0.0625, 16.0


def device(z, c, y, x):
    return (z * NC + c) * (NY * NX) + y * NX + x


def exchange(value, axis, stage):
    pairs = []
    for z in range(NZ):
        for c in range(NC):
            u = 1 if (stage + c) % 2 == 0 else 3
            for y in range(NY):
                for x in range(NX):
                    to = {
                        "z": (z ^ u, c, y, x),
                        "y": (z, c, y ^ u, x),
                        "x": (z, c, y, x ^ u),
                        "core": (z, 1 - c, y, x),
                    }[axis]
                    pairs.append((device(z, c, y, x), device(*to)))
    return lax.ppermute(value, AXES, pairs)


def tables():
    out = np.zeros((NZ * NC * NY * NX, 48), np.int32)
    for z in range(NZ):
        for c in range(NC):
            u, v = (1, 3) if c == 0 else (3, 1)
            first, second = (2, u, v, 0), (u, 2, 0, v)
            for y in range(NY):
                for x in range(NX):
                    row = [(y ^ j) * NX + (x ^ i) for i in first for j in second]
                    row += [(y ^ i) * NX + (x ^ j) for i in first for j in second]
                    row += [(z ^ i) * NC + c for i in (0, u, v, 2)]
                    row += [(z ^ i) * NC + 1 - c for i in (0, v, u, 2)]
                    out[device(z, c, y, x), : len(row)] = row
    return out


def relay_kernel(head, out):
    out[...] = jnp.swapaxes(head[...], 0, 1)


def relay(head, start, count, step=64):
    _, n_a, c = head.shape
    return pl.pallas_call(
        relay_kernel,
        grid=(count // step,),
        in_specs=[pl.BlockSpec((step, n_a, c), lambda i: (start // step + i, 0, 0))],
        out_specs=pl.BlockSpec((n_a, step, c), lambda i: (0, i, 0)),
        out_shape=jax.ShapeDtypeStruct((n_a, count, c), head.dtype),
        compiler_params=pltpu.CompilerParams(vmem_limit_bytes=12 << 20),
        cost_estimate=pl.CostEstimate(flops=10**10, bytes_accessed=2**24, transcendentals=0),
    )(head)


def matmul_kernel(table, alpha, xb0, xb1, xe, xa, wb0, wb1, we, wa, *rest):
    out = rest[-1]
    base0, base1, expert, anti = [
        jnp.dot(x[...], w[0], preferred_element_type=F32)
        for x, w in ((xb0, wb0), (xb1, wb1), (xe, we), (xa, wa))
    ]
    total = base0 + base1 + alpha[0] * (expert - anti)
    for arrived in rest[:-1]:
        total += arrived[0].astype(F32)
    out[0] = total.astype(out.dtype)


def project(table, alpha, acts, heads, first, half, dtype, *arrived):
    tokens = acts.shape[0]
    half_c = heads[0].shape[2] // 2
    quarter = heads[0].shape[1]

    def features(i):
        return pl.BlockSpec((tokens, quarter), lambda _, tab: (0, i))

    def weights():
        return pl.BlockSpec((1, quarter, half_c), lambda i, tab: (tab[first + i], 0, half))

    block = pl.BlockSpec((1, tokens, half_c), lambda i, tab: (i, 0, 0))
    return pl.pallas_call(
        matmul_kernel,
        grid_spec=pltpu.PrefetchScalarGridSpec(
            num_scalar_prefetch=1,
            grid=(4,),
            in_specs=[pl.BlockSpec(memory_space=pltpu.SMEM)]
            + [features(i) for i in range(4)]
            + [weights() for _ in heads]
            + [block for _ in arrived],
            out_specs=block,
        ),
        out_shape=jax.ShapeDtypeStruct((4, tokens, half_c), dtype),
        compiler_params=pltpu.CompilerParams(vmem_limit_bytes=12 << 20),
        cost_estimate=pl.CostEstimate(flops=1, bytes_accessed=1, transcendentals=0),
    )(table, alpha, *[acts] * 4, *heads, *arrived)


def wide(value):
    return value.astype(F32) * UP if value.dtype == F16 else value.astype(F32)


def narrow(value):
    return (value * DOWN).astype(F16)


def in_hbm(value):
    return pltpu.with_memory_space_constraint(value, pltpu.HBM)


def together(*values):
    return lax.optimization_barrier(values)


def lanes(columns, rows):
    lane = lax.broadcasted_iota(jnp.int32, (rows, 128), 1)
    out = jnp.zeros((rows, 128), F32)
    for i, column in enumerate(columns):
        out = jnp.where(lane == i, column, out)
    return out


def to_all(out, columns):
    rows = columns[0].shape[0]
    square = jnp.concatenate([lanes(columns, rows), jnp.zeros((128 - rows, 128), F32)])
    out[...] = jnp.broadcast_to(square.T[None, :8], out.shape)


def square_kernel(*refs):
    values = [h[...].astype(F32) for h in refs[:-1]]
    sums = [jnp.sum(h * h, axis=1, keepdims=True) for h in values]
    refs[-1][...] = lanes(sums, refs[-1].shape[0])


def norm_kernel(widths, *refs):
    hidden, gains, sq, got, out = refs[:3], refs[3:6], refs[6], refs[7], refs[8]
    total = sq[...] + got[...]
    at = 0
    for i, h in enumerate(hidden):
        scale = lax.rsqrt(total[:, i : i + 1] / widths[i] + 1e-05)
        value = h[...].astype(F32) * scale * gains[i][...].astype(F32)
        out[:, at : at + h.shape[1]] = value.astype(out.dtype)
        at += h.shape[1]


def join_kernel(source, mine, other, out):
    rows = mine.shape[0] // NZ
    for j in range(NZ * NC):
        ref, first = (mine, j * rows) if j < NZ else (other, (j - NZ) * rows)
        out[pl.ds(pl.multiple_of(source[j] * rows, rows), rows)] = ref[first : first + rows]


def stats_kernel(home, wanted, out):
    pieces, rows, width = home.shape
    top = jnp.max(home[...], axis=(0,))
    top = jnp.max(top, axis=1, keepdims=True)
    total = jnp.zeros((rows, width), F32)
    pick = jnp.zeros((rows, width), F32)
    lane = lax.broadcasted_iota(jnp.int32, (rows, width), 1)
    for i in range(pieces):
        value = home[i]
        total += jnp.exp(value - top)
        pick += jnp.where(lane == wanted[...] - i * width, value, 0.0)
    total = jnp.sum(total, axis=1, keepdims=True)
    pick = jnp.sum(pick, axis=1, keepdims=True)
    to_all(out, [top, total, pick])


def final_kernel(home, stats, out, picked):
    pieces, rows, width = home.shape
    tops, totals, picks = [stats[:, i, :rows] for i in range(3)]
    top = jnp.max(tops, axis=0, keepdims=True)
    logz = top + jnp.log(jnp.sum(totals * jnp.exp(tops - top), axis=0, keepdims=True))
    picked[...] = jnp.sum(picks, axis=0, keepdims=True) - logz
    square = jnp.concatenate(
        [jnp.broadcast_to(logz, (128, rows)), jnp.zeros((128, 128 - rows), F32)], axis=1
    )
    column = square.T[:rows, :1]
    for i in range(pieces):
        out[:, i * width : (i + 1) * width] = home[i] - column


def call(kernel, shapes, *args):
    def spec(v):
        small = v.ndim == 1 and v.dtype == jnp.int32
        return pl.BlockSpec(memory_space=pltpu.SMEM) if small else pl.BlockSpec()

    outs = [jax.ShapeDtypeStruct(s, d) for s, d in shapes]
    result = pl.pallas_call(
        kernel,
        in_specs=[spec(v) for v in args],
        out_specs=[pl.BlockSpec() for _ in outs],
        out_shape=outs,
        compiler_params=pltpu.CompilerParams(vmem_limit_bytes=16 << 20),
    )(*args)
    return result if len(outs) > 1 else result[0]


def shards(
    base_hidden,
    expert_hidden,
    anti_hidden,
    base_gain,
    expert_gain,
    anti_gain,
    base_head,
    expert_head,
    anti_head,
    strength,
    token_ids,
):
    r = lax.axis_index("rows")
    t = lax.axis_index("tensor")
    rows, c_width = token_ids.shape[0], base_head.shape[2]
    mine = lax.dynamic_slice(jnp.asarray(tables()), (r * (NY * NX) + t, 0), (1, 48))[0]
    table, source = mine[:32], mine[32:40]

    quarter = expert_head.shape[0]
    heads = []

    def swap(value, axis, stage, *beside):
        ready = together(value, *[head for head, _ in beside])
        done = [relay(h, start, quarter) for h, (_, start) in zip(ready[1:], beside)]
        got, *done = together(exchange(ready[0], axis, stage), *done)
        heads.extend(done)
        return got

    hidden = (base_hidden, expert_hidden, anti_hidden)
    gains = [g[None] for g in (base_gain, expert_gain, anti_gain)]
    width = sum(h.shape[1] for h in hidden)
    flat = [in_hbm(h) for h in hidden]
    sq = call(square_kernel, [((rows, 128), F32)], *flat)
    sq += exchange(sq, "x", 0)
    sq += exchange(sq, "x", 1)
    sq += exchange(sq, "y", 0)
    got = exchange(sq, "y", 1)
    normed = call(
        functools.partial(norm_kernel, (D, DE, DE)), [((rows, width), BF)], *flat, *gains, sq, got
    )
    pair = swap(normed, "z", 0, (expert_head, 0), (anti_head, 0))
    far = swap(jnp.stack([normed, pair]), "z", 1, (base_head, 0), (base_head, quarter))
    mine = jnp.concatenate([normed, pair, far[0], far[1]])
    other = exchange(mine, "core", 0)
    heads = heads[2:] + heads[:2]
    acts = call(join_kernel, [((NZ * NC * rows, width), BF)], source, mine, other)

    axes = (("x", "y"), ("y", "x"))
    kept = [[], []]
    moved = [[], []]
    for i in range(4):
        for half in range(2):
            kind = BF if i < 2 else F32
            arrived = moved[half][1:] if i == 3 else []
            part = project(table, strength, acts, heads, 16 * half + 4 * i, half, kind, *arrived)
            table, part = together(table, part)
            if i < 2:
                moved[half].append(exchange(part, axes[half][0], 0))
            else:
                kept[half].append(part)
    second_step = [
        exchange(narrow(kept[h][0] + wide(moved[h][0])), axes[h][0], 1) for h in range(2)
    ]
    sums = [kept[h][1] + wide(second_step[h]) for h in range(2)]
    moved = [exchange(narrow(sums[h][:2]), axes[h][1], 0) for h in range(2)]
    second_step = [
        exchange(narrow(sums[h][3] + wide(moved[h][1])), axes[h][1], 1) for h in range(2)
    ]
    logits = jnp.concatenate(
        [narrow(sums[h][2] + wide(moved[h][0]) + wide(second_step[h])) for h in range(2)], axis=1
    ).reshape(NZ * NC, rows, c_width)

    home = wide(lax.all_to_all(logits, "rows", 0, 0, tiled=True))
    wanted = (token_ids - t * (8 * c_width))[:, None]
    stats = call(stats_kernel, [((NY * NX, 8, 128), F32)], home, wanted)
    stats = lax.all_to_all(stats, "tensor", 0, 0, tiled=True)
    log_probs, picked = call(
        final_kernel, [((rows, 8 * c_width), F32), ((1, rows), F32)], home, stats
    )
    return log_probs, picked[0]


def solution(mesh):
    return jax.shard_map(
        shards,
        mesh=mesh,
        in_specs=(
            P("rows", "tensor"),
            P("rows", "tensor"),
            P("rows", "tensor"),
            P("tensor"),
            P("tensor"),
            P("tensor"),
            P("tensor", None, "rows"),
            P("tensor", None, "rows"),
            P("tensor", None, "rows"),
            P(),
            P("rows"),
        ),
        out_specs=(P("rows", "tensor"), P("rows")),
        check_vma=False,
    )
```

```python
import functools

import jax
import jax.numpy as jnp
import numpy as np
from jax import lax
from jax.experimental import pallas as pl
from jax.experimental.pallas import tpu as pltpu
from jax.sharding import PartitionSpec as P

D = 8192
DE = 4096
NZ, NC, NY, NX = 4, 2, 4, 4
AXES = ("rows", "tensor")
BF = jnp.bfloat16
F16 = jnp.float16
F32 = jnp.float32
DOWN, UP = 0.0625, 16.0


def device(z, c, y, x):
    return (z * NC + c) * (NY * NX) + y * NX + x


def exchange(value, axis, stage):
    pairs = []
    for z in range(NZ):
        for c in range(NC):
            u = 1 if (stage + c) % 2 == 0 else 3
            for y in range(NY):
                for x in range(NX):
                    to = {
                        "z": (z ^ u, c, y, x),
                        "y": (z, c, y ^ u, x),
                        "x": (z, c, y, x ^ u),
                        "core": (z, 1 - c, y, x),
                    }[axis]
                    pairs.append((device(z, c, y, x), device(*to)))
    return lax.ppermute(value, AXES, pairs)


def tables():
    out = np.zeros((NZ * NC * NY * NX, 48), np.int32)
    for z in range(NZ):
        for c in range(NC):
            u, v = (1, 3) if c == 0 else (3, 1)
            first, second = (2, u, v, 0), (u, 2, 0, v)
            for y in range(NY):
                for x in range(NX):
                    row = [(y ^ j) * NX + (x ^ i) for i in first for j in second]
                    row += [(y ^ i) * NX + (x ^ j) for i in first for j in second]
                    row += [(z ^ i) * NC + c for i in (0, u, v, 2)]
                    row += [(z ^ i) * NC + 1 - c for i in (0, v, u, 2)]
                    out[device(z, c, y, x), : len(row)] = row
    return out


def relay_kernel(head, out):
    out[...] = jnp.swapaxes(head[...], 0, 1)


def relay(head, start, count, step=64):
    _, n_a, c = head.shape
    return pl.pallas_call(
        relay_kernel,
        grid=(count // step,),
        in_specs=[pl.BlockSpec((step, n_a, c), lambda i: (start // step + i, 0, 0))],
        out_specs=pl.BlockSpec((n_a, step, c), lambda i: (0, i, 0)),
        out_shape=jax.ShapeDtypeStruct((n_a, count, c), head.dtype),
        compiler_params=pltpu.CompilerParams(vmem_limit_bytes=12 << 20),
        cost_estimate=pl.CostEstimate(flops=10**10, bytes_accessed=2**24, transcendentals=0),
    )(head)


def matmul_kernel(first, half, table, alpha, acts, wb0, wb1, we, wa, *rest):
    out = rest[-1]
    quarter, cols = wb0.shape[1], out.shape[2]
    for i in range(out.shape[0]):
        block = table[first + i]
        base0, base1, expert, anti = [
            jnp.dot(
                acts[:, j * quarter : (j + 1) * quarter],
                w[block, :, half * cols : (half + 1) * cols],
                preferred_element_type=F32,
            )
            for j, w in enumerate((wb0, wb1, we, wa))
        ]
        total = base0 + base1 + alpha[0] * (expert - anti)
        for arrived in rest[:-1]:
            total += arrived[i].astype(F32)
        out[i] = total.astype(out.dtype)


def project(table, alpha, acts, heads, first, half, dtype, *arrived):
    smem = pl.BlockSpec(memory_space=pltpu.SMEM)
    vmem = pl.BlockSpec(memory_space=pltpu.VMEM)
    args = (table, alpha, acts, *heads, *arrived)
    return pl.pallas_call(
        functools.partial(matmul_kernel, first, half),
        in_specs=[smem] * 2 + [vmem] * (len(args) - 2),
        out_specs=vmem,
        out_shape=jax.ShapeDtypeStruct((4, acts.shape[0], heads[0].shape[2] // 2), dtype),
        compiler_params=pltpu.CompilerParams(vmem_limit_bytes=12 << 20),
        cost_estimate=pl.CostEstimate(flops=1, bytes_accessed=1, transcendentals=0),
    )(*args)


def wide(value):
    return value.astype(F32) * UP if value.dtype == F16 else value.astype(F32)


def narrow(value):
    return (value * DOWN).astype(F16)


def in_hbm(value):
    return pltpu.with_memory_space_constraint(value, pltpu.HBM)


def together(*values):
    return lax.optimization_barrier(values)


def lanes(columns, rows):
    lane = lax.broadcasted_iota(jnp.int32, (rows, 128), 1)
    out = jnp.zeros((rows, 128), F32)
    for i, column in enumerate(columns):
        out = jnp.where(lane == i, column, out)
    return out


def to_all(out, columns):
    rows = columns[0].shape[0]
    square = jnp.concatenate([lanes(columns, rows), jnp.zeros((128 - rows, 128), F32)])
    out[...] = jnp.broadcast_to(square.T[None, :8], out.shape)


def square_kernel(*refs):
    values = [h[...].astype(F32) for h in refs[:-1]]
    to_all(refs[-1], [jnp.sum(h * h, axis=1, keepdims=True) for h in values])


def norm_kernel(widths, *refs):
    hidden, gains, sums, out = refs[:3], refs[3:6], refs[6], refs[7]
    total = jnp.sum(sums[...], axis=0)
    total = jnp.concatenate([total, jnp.zeros((120, 128), F32)]).T[: out.shape[0]]
    at = 0
    for i, h in enumerate(hidden):
        scale = lax.rsqrt(total[:, i : i + 1] / widths[i] + 1e-05)
        value = h[...].astype(F32) * scale * gains[i][...].astype(F32)[None]
        out[:, at : at + h.shape[1]] = value.astype(out.dtype)
        at += h.shape[1]


def join_kernel(source, mine, other, out):
    rows = mine.shape[0] // NZ
    for j in range(NZ * NC):
        ref, first = (mine, j * rows) if j < NZ else (other, (j - NZ) * rows)
        out[pl.ds(pl.multiple_of(source[j] * rows, rows), rows)] = ref[first : first + rows]


def stats_kernel(home, wanted, out):
    pieces, rows, width = home.shape
    top = jnp.max(home[...], axis=(0,))
    top = jnp.max(top, axis=1, keepdims=True)
    total = jnp.zeros((rows, width), F32)
    pick = jnp.zeros((rows, width), F32)
    lane = lax.broadcasted_iota(jnp.int32, (rows, width), 1)
    for i in range(pieces):
        value = home[i]
        total += jnp.exp(value - top)
        pick += jnp.where(lane == wanted[...] - i * width, value, 0.0)
    total = jnp.sum(total, axis=1, keepdims=True)
    pick = jnp.sum(pick, axis=1, keepdims=True)
    to_all(out, [top, total, pick])


def final_kernel(home, stats, out, picked):
    pieces, rows, width = home.shape
    tops, totals, picks = [stats[:, i, :rows] for i in range(3)]
    top = jnp.max(tops, axis=0, keepdims=True)
    logz = top + jnp.log(jnp.sum(totals * jnp.exp(tops - top), axis=0, keepdims=True))
    picked[...] = jnp.sum(picks, axis=0, keepdims=True) - logz
    square = jnp.concatenate(
        [jnp.broadcast_to(logz, (128, rows)), jnp.zeros((128, 128 - rows), F32)], axis=1
    )
    column = square.T[:rows, :1]
    for i in range(pieces):
        out[:, i * width : (i + 1) * width] = home[i] - column


def call(kernel, shapes, *args):
    def spec(v):
        small = v.ndim == 1 and v.dtype == jnp.int32
        return pl.BlockSpec(memory_space=pltpu.SMEM) if small else pl.BlockSpec()

    outs = [jax.ShapeDtypeStruct(s, d) for s, d in shapes]
    result = pl.pallas_call(
        kernel,
        in_specs=[spec(v) for v in args],
        out_specs=[pl.BlockSpec() for _ in outs],
        out_shape=outs,
        compiler_params=pltpu.CompilerParams(vmem_limit_bytes=16 << 20),
    )(*args)
    return result if len(outs) > 1 else result[0]


def shards(
    base_hidden,
    expert_hidden,
    anti_hidden,
    base_gain,
    expert_gain,
    anti_gain,
    base_head,
    expert_head,
    anti_head,
    strength,
    token_ids,
):
    r = lax.axis_index("rows")
    t = lax.axis_index("tensor")
    rows, c_width = token_ids.shape[0], base_head.shape[2]
    mine = lax.dynamic_slice(jnp.asarray(tables()), (r * (NY * NX) + t, 0), (1, 48))[0]
    table, source = mine[:32], mine[32:40]

    quarter = expert_head.shape[0]
    heads = []

    def swap(value, axis, stage, *beside):
        ready = together(value, *[head for head, _ in beside])
        done = [relay(h, start, quarter) for h, (_, start) in zip(ready[1:], beside)]
        got, *done = together(exchange(ready[0], axis, stage), *done)
        heads.extend(done)
        return got

    hidden = (base_hidden, expert_hidden, anti_hidden)
    gains = [in_hbm(g) for g in (base_gain, expert_gain, anti_gain)]
    width = sum(h.shape[1] for h in hidden)
    flat = [in_hbm(h) for h in hidden]
    sums = call(square_kernel, [((NY * NX, 8, 128), F32)], *flat)
    sums = lax.all_to_all(sums, "tensor", 0, 0, tiled=True)
    normed = call(
        functools.partial(norm_kernel, (D, DE, DE)), [((rows, width), BF)], *flat, *gains, sums
    )
    pair = swap(normed, "z", 0, (expert_head, 0), (anti_head, 0))
    far = swap(jnp.stack([normed, pair]), "z", 1, (base_head, 0), (base_head, quarter))
    mine = jnp.concatenate([normed, pair, far[0], far[1]])
    other = exchange(mine, "core", 0)
    heads = heads[2:] + heads[:2]
    acts = call(join_kernel, [((NZ * NC * rows, width), BF)], source, mine, other)

    axes = (("x", "y"), ("y", "x"))
    kept = [[], []]
    moved = [[], []]
    for i in range(4):
        for half in range(2):
            kind = BF if i < 2 else F32
            arrived = moved[half][1:] if i == 3 else []
            part = project(table, strength, acts, heads, 16 * half + 4 * i, half, kind, *arrived)
            table, part = together(table, part)
            if i < 2:
                moved[half].append(exchange(part, axes[half][0], 0))
            else:
                kept[half].append(part)
    second_step = [
        exchange(narrow(kept[h][0] + wide(moved[h][0])), axes[h][0], 1) for h in range(2)
    ]
    sums = [kept[h][1] + wide(second_step[h]) for h in range(2)]
    moved = [exchange(narrow(sums[h][:2]), axes[h][1], 0) for h in range(2)]
    second_step = [
        exchange(narrow(sums[h][3] + wide(moved[h][1])), axes[h][1], 1) for h in range(2)
    ]
    logits = jnp.concatenate(
        [narrow(sums[h][2] + wide(moved[h][0]) + wide(second_step[h])) for h in range(2)], axis=1
    ).reshape(NZ * NC, rows, c_width)

    home = wide(lax.all_to_all(logits, "rows", 0, 0, tiled=True))
    wanted = (token_ids - t * (8 * c_width))[:, None]
    stats = call(stats_kernel, [((NY * NX, 8, 128), F32)], home, wanted)
    stats = lax.all_to_all(stats, "tensor", 0, 0, tiled=True)
    log_probs, picked = call(
        final_kernel, [((rows, 8 * c_width), F32), ((1, rows), F32)], home, stats
    )
    return log_probs, picked[0]


def solution(mesh):
    return jax.shard_map(
        shards,
        mesh=mesh,
        in_specs=(
            P("rows", "tensor"),
            P("rows", "tensor"),
            P("rows", "tensor"),
            P("tensor"),
            P("tensor"),
            P("tensor"),
            P("tensor", None, "rows"),
            P("tensor", None, "rows"),
            P("tensor", None, "rows"),
            P(),
            P("rows"),
        ),
        out_specs=(P("rows", "tensor"), P("rows")),
        check_vma=False,
    )
```

```python
import functools

import jax
import jax.numpy as jnp
import numpy as np
from jax import lax
from jax.experimental import pallas as pl
from jax.experimental.pallas import tpu as pltpu
from jax.sharding import PartitionSpec as P

D = 8192
DE = 4096
NZ, NC, NY, NX = 4, 2, 4, 4
AXES = ("rows", "tensor")
BF = jnp.bfloat16
F16 = jnp.float16
F32 = jnp.float32
DOWN, UP = 0.0625, 16.0
ALONG_Z = (1, 3, 2)


def device(z, c, y, x):
    return (z * NC + c) * (NY * NX) + y * NX + x


def exchange(value, axis, stage=0, by=None):
    pairs = []
    for z in range(NZ):
        for c in range(NC):
            u = by or (1 if (stage + c) % 2 == 0 else 3)
            for y in range(NY):
                for x in range(NX):
                    to = {
                        "z": (z ^ u, c, y, x),
                        "y": (z, c, y ^ u, x),
                        "x": (z, c, y, x ^ u),
                        "core": (z, 1 - c, y, x),
                    }[axis]
                    pairs.append((device(z, c, y, x), device(*to)))
    return lax.ppermute(value, AXES, pairs)


def tables():
    out = np.zeros((NZ * NC * NY * NX, 48), np.int32)
    for z in range(NZ):
        for c in range(NC):
            u, v = (1, 3) if c == 0 else (3, 1)
            first, second = (2, u, v, 0), (u, 2, 0, v)
            for y in range(NY):
                for x in range(NX):
                    row = [(y ^ j) * NX + (x ^ i) for i in first for j in second]
                    row += [(y ^ i) * NX + (x ^ j) for i in first for j in second]
                    row += [(z ^ i) * NC + k for i in (0,) + ALONG_Z for k in (c, 1 - c)]
                    out[device(z, c, y, x), : len(row)] = row
    return out


def relay_kernel(head, out):
    out[...] = jnp.swapaxes(head[...], 0, 1)


def relay(head, start, count, step=64):
    _, n_a, c = head.shape
    return pl.pallas_call(
        relay_kernel,
        grid=(count // step,),
        in_specs=[pl.BlockSpec((step, n_a, c), lambda i: (start // step + i, 0, 0))],
        out_specs=pl.BlockSpec((n_a, step, c), lambda i: (0, i, 0)),
        out_shape=jax.ShapeDtypeStruct((n_a, count, c), head.dtype),
        compiler_params=pltpu.CompilerParams(vmem_limit_bytes=12 << 20),
        cost_estimate=pl.CostEstimate(flops=10**10, bytes_accessed=2**24, transcendentals=0),
    )(head)


def matmul_kernel(first, half, table, alpha, acts, wb0, wb1, we, wa, *rest):
    out = rest[-1]
    quarter, cols = wb0.shape[1], out.shape[2]
    for i in range(out.shape[0]):
        block = table[first + i]
        base0, base1, expert, anti = [
            jnp.dot(
                acts[:, j * quarter : (j + 1) * quarter],
                w[block, :, half * cols : (half + 1) * cols],
                preferred_element_type=F32,
            )
            for j, w in enumerate((wb0, wb1, we, wa))
        ]
        total = base0 + base1 + alpha[0] * (expert - anti)
        for arrived in rest[:-1]:
            total += arrived[i].astype(F32)
        out[i] = total.astype(out.dtype)


def project(table, alpha, acts, heads, first, half, dtype, *arrived):
    smem = pl.BlockSpec(memory_space=pltpu.SMEM)
    vmem = pl.BlockSpec(memory_space=pltpu.VMEM)
    args = (table, alpha, acts, *heads, *arrived)
    return pl.pallas_call(
        functools.partial(matmul_kernel, first, half),
        in_specs=[smem] * 2 + [vmem] * (len(args) - 2),
        out_specs=vmem,
        out_shape=jax.ShapeDtypeStruct((4, acts.shape[0], heads[0].shape[2] // 2), dtype),
        compiler_params=pltpu.CompilerParams(vmem_limit_bytes=12 << 20),
        cost_estimate=pl.CostEstimate(flops=1, bytes_accessed=1, transcendentals=0),
    )(*args)


def wide(value):
    return value.astype(F32) * UP if value.dtype == F16 else value.astype(F32)


def narrow(value):
    return (value * DOWN).astype(F16)


def in_hbm(value):
    return pltpu.with_memory_space_constraint(value, pltpu.HBM)


def together(*values):
    return lax.optimization_barrier(values)


def lanes(columns, rows):
    lane = lax.broadcasted_iota(jnp.int32, (rows, 128), 1)
    out = jnp.zeros((rows, 128), F32)
    for i, column in enumerate(columns):
        out = jnp.where(lane == i, column, out)
    return out


def to_all(out, columns):
    rows = columns[0].shape[0]
    square = jnp.concatenate([lanes(columns, rows), jnp.zeros((128 - rows, 128), F32)])
    out[...] = jnp.broadcast_to(square.T[None, :8], out.shape)


def square_kernel(*refs):
    values = [h[...].astype(F32) for h in refs[:-1]]
    to_all(refs[-1], [jnp.sum(h * h, axis=1, keepdims=True) for h in values])


def norm_kernel(widths, *refs):
    hidden, gains, sums, out = refs[:3], refs[3:6], refs[6], refs[7]
    total = jnp.sum(sums[...], axis=0)
    total = jnp.concatenate([total, jnp.zeros((120, 128), F32)]).T[: out.shape[0]]
    at = 0
    for i, h in enumerate(hidden):
        scale = lax.rsqrt(total[:, i : i + 1] / widths[i] + 1e-05)
        value = h[...].astype(F32) * scale * gains[i][...].astype(F32)[None]
        out[:, at : at + h.shape[1]] = value.astype(out.dtype)
        at += h.shape[1]


def join_kernel(*refs):
    at = 0
    for ref in refs[:-1]:
        refs[-1][at : at + ref.shape[0]] = ref[...]
        at += ref.shape[0]


def stats_kernel(source, home, wanted, out):
    pieces, rows, width = home.shape
    top = jnp.max(home[...], axis=(0,))
    top = jnp.max(top, axis=1, keepdims=True)
    total = jnp.zeros((rows, width), F32)
    pick = jnp.zeros((rows, width), F32)
    lane = lax.broadcasted_iota(jnp.int32, (rows, width), 1)
    for i in range(pieces):
        value = home[i]
        total += jnp.exp(value - top)
        pick += jnp.where(lane == wanted[...] - source[i] * width, value, 0.0)
    total = jnp.sum(total, axis=1, keepdims=True)
    pick = jnp.sum(pick, axis=1, keepdims=True)
    to_all(out, [top, total, pick])


def final_kernel(source, home, stats, out, picked):
    pieces, rows, width = home.shape
    tops, totals, picks = [stats[:, i, :rows] for i in range(3)]
    top = jnp.max(tops, axis=0, keepdims=True)
    logz = top + jnp.log(jnp.sum(totals * jnp.exp(tops - top), axis=0, keepdims=True))
    picked[...] = jnp.sum(picks, axis=0, keepdims=True) - logz
    square = jnp.concatenate(
        [jnp.broadcast_to(logz, (128, rows)), jnp.zeros((128, 128 - rows), F32)], axis=1
    )
    column = square.T[:rows, :1]
    for i in range(pieces):
        at = pl.multiple_of(source[i] * width, width)
        out[:, pl.ds(at, width)] = home[i] - column


def call(kernel, shapes, *args):
    def spec(v):
        small = v.ndim == 1 and v.dtype == jnp.int32
        return pl.BlockSpec(memory_space=pltpu.SMEM) if small else pl.BlockSpec()

    outs = [jax.ShapeDtypeStruct(s, d) for s, d in shapes]
    result = pl.pallas_call(
        kernel,
        in_specs=[spec(v) for v in args],
        out_specs=[pl.BlockSpec() for _ in outs],
        out_shape=outs,
        compiler_params=pltpu.CompilerParams(vmem_limit_bytes=16 << 20),
    )(*args)
    return result if len(outs) > 1 else result[0]


def shards(
    base_hidden,
    expert_hidden,
    anti_hidden,
    base_gain,
    expert_gain,
    anti_gain,
    base_head,
    expert_head,
    anti_head,
    strength,
    token_ids,
):
    r = lax.axis_index("rows")
    t = lax.axis_index("tensor")
    rows, c_width = token_ids.shape[0], base_head.shape[2]
    mine = lax.dynamic_slice(jnp.asarray(tables()), (r * (NY * NX) + t, 0), (1, 48))[0]
    table, source = mine[:32], mine[32:40]

    quarter = expert_head.shape[0]
    heads = []

    def swap(value, moves, *beside):
        ready = together(value, *[head for head, _ in beside])
        got = [exchange(ready[0], *move) for move in moves]
        done = [relay(h, start, quarter) for h, (_, start) in zip(ready[1:], beside)]
        results = together(*got, *done)
        heads.extend(results[len(moves) :])
        return results[: len(moves)]

    hidden = (base_hidden, expert_hidden, anti_hidden)
    gains = [in_hbm(g) for g in (base_gain, expert_gain, anti_gain)]
    width = sum(h.shape[1] for h in hidden)
    flat = [in_hbm(h) for h in hidden]
    sums = call(square_kernel, [((NY * NX, 8, 128), F32)], *flat)
    sums = lax.all_to_all(sums, "tensor", 0, 0, tiled=True)
    normed = call(
        functools.partial(norm_kernel, (D, DE, DE)), [((rows, width), BF)], *flat, *gains, sums
    )
    along_z = [("z", 0, k) for k in ALONG_Z]
    got = swap(normed, along_z, (expert_head, 0), (base_head, 0), (base_head, quarter))
    mine = jnp.concatenate([normed, *got])
    (other,) = swap(mine, [("core",)], (anti_head, 0))
    heads = heads[1:3] + [heads[0], heads[3]]
    acts = call(join_kernel, [((NZ * NC * rows, width), BF)], mine, other)

    axes = (("x", "y"), ("y", "x"))
    kept = [[], []]
    moved = [[], []]
    for i in range(4):
        for half in range(2):
            kind = BF if i < 2 else F32
            arrived = moved[half][1:] if i == 3 else []
            part = project(table, strength, acts, heads, 16 * half + 4 * i, half, kind, *arrived)
            table, part = together(table, part)
            if i < 2:
                moved[half].append(exchange(part, axes[half][0], 0))
            else:
                kept[half].append(part)
    second_step = [
        exchange(narrow(kept[h][0] + wide(moved[h][0])), axes[h][0], 1) for h in range(2)
    ]
    sums = [kept[h][1] + wide(second_step[h]) for h in range(2)]
    moved = [exchange(narrow(sums[h][:2]), axes[h][1], 0) for h in range(2)]
    second_step = [
        exchange(narrow(sums[h][3] + wide(moved[h][1])), axes[h][1], 1) for h in range(2)
    ]
    logits = jnp.concatenate(
        [narrow(sums[h][2] + wide(moved[h][0]) + wide(second_step[h])) for h in range(2)], axis=1
    ).reshape(NC, NZ, rows, c_width)

    other = exchange(logits[1], "core")
    both = [jnp.stack([logits[0, i], other[i]]) for i in range(NZ)]
    home = [both[0]] + [exchange(m, *move) for m, move in zip(both[1:], along_z)]
    home = wide(jnp.concatenate(home))

    wanted = (token_ids - t * (8 * c_width))[:, None]
    stats = call(stats_kernel, [((NY * NX, 8, 128), F32)], source, home, wanted)
    stats = lax.all_to_all(stats, "tensor", 0, 0, tiled=True)
    log_probs, picked = call(
        final_kernel, [((rows, 8 * c_width), F32), ((1, rows), F32)], source, home, stats
    )
    return log_probs, picked[0]


def solution(mesh):
    return jax.shard_map(
        shards,
        mesh=mesh,
        in_specs=(
            P("rows", "tensor"),
            P("rows", "tensor"),
            P("rows", "tensor"),
            P("tensor"),
            P("tensor"),
            P("tensor"),
            P("tensor", None, "rows"),
            P("tensor", None, "rows"),
            P("tensor", None, "rows"),
            P(),
            P("rows"),
        ),
        out_specs=(P("rows", "tensor"), P("rows")),
        check_vma=False,
    )
```

```python
import functools

import jax
import jax.numpy as jnp
import numpy as np
from jax import lax
from jax.experimental import pallas as pl
from jax.experimental.pallas import tpu as pltpu
from jax.sharding import PartitionSpec as P

D = 8192
DE = 4096
VOCAB = 65536
NZ, NC, NY, NX = 4, 2, 4, 4
AXES = ("rows", "tensor")
BF = jnp.bfloat16
F16 = jnp.float16
F32 = jnp.float32
DOWN, UP = 0.0625, 16.0
ALONG_Z = (1, 3, 2)


def device(z, c, y, x):
    return (z * NC + c) * (NY * NX) + y * NX + x


def exchange(value, axis, stage=0, by=None):
    pairs = []
    for z in range(NZ):
        for c in range(NC):
            u = by or (1 if (stage + c) % 2 == 0 else 3)
            for y in range(NY):
                for x in range(NX):
                    to = {
                        "z": (z ^ u, c, y, x),
                        "y": (z, c, y ^ u, x),
                        "x": (z, c, y, x ^ u),
                        "core": (z, 1 - c, y, x),
                    }[axis]
                    pairs.append((device(z, c, y, x), device(*to)))
    return lax.ppermute(value, AXES, pairs)


def tables():
    out = np.zeros((NZ * NC * NY * NX, 48), np.int32)
    for z in range(NZ):
        for c in range(NC):
            u, v = (1, 3) if c == 0 else (3, 1)
            first, second = (2, u, v, 0), (u, 2, 0, v)
            for y in range(NY):
                for x in range(NX):
                    row = [(y ^ j) * NX + (x ^ i) for i in first for j in second]
                    row += [(y ^ i) * NX + (x ^ j) for i in first for j in second]
                    row += [(z ^ i) * NC + k for i in (0,) + ALONG_Z for k in (c, 1 - c)]
                    row += [(y * NX + x) * (VOCAB // (NY * NX))]
                    out[device(z, c, y, x), : len(row)] = row
    return out


def relay_kernel(head, out):
    out[...] = jnp.swapaxes(head[...], 0, 1)


def relay(head, start, count, step=64):
    _, n_a, c = head.shape
    return pl.pallas_call(
        relay_kernel,
        grid=(count // step,),
        in_specs=[pl.BlockSpec((step, n_a, c), lambda i: (start // step + i, 0, 0))],
        out_specs=pl.BlockSpec((n_a, step, c), lambda i: (0, i, 0)),
        out_shape=jax.ShapeDtypeStruct((n_a, count, c), head.dtype),
        compiler_params=pltpu.CompilerParams(vmem_limit_bytes=12 << 20),
        cost_estimate=pl.CostEstimate(flops=10**10, bytes_accessed=2**24, transcendentals=0),
    )(head)


def matmul_kernel(first, half, table, alpha, acts, wb0, wb1, we, wa, out):
    quarter, cols = wb0.shape[1], out.shape[2]
    for i in range(out.shape[0]):
        block = table[first + i]
        base0, base1, expert, anti = [
            jnp.dot(
                acts[:, j * quarter : (j + 1) * quarter],
                w[block, :, half * cols : (half + 1) * cols],
                preferred_element_type=F32,
            )
            for j, w in enumerate((wb0, wb1, we, wa))
        ]
        total = base0 + base1 + alpha[0] * (expert - anti)
        out[i] = total.astype(out.dtype)


def project(table, alpha, acts, heads, first, half, dtype):
    smem = pl.BlockSpec(memory_space=pltpu.SMEM)
    vmem = pl.BlockSpec(memory_space=pltpu.VMEM)
    args = (table, alpha, acts, *heads)
    return pl.pallas_call(
        functools.partial(matmul_kernel, first, half),
        in_specs=[smem] * 2 + [vmem] * (len(args) - 2),
        out_specs=vmem,
        out_shape=jax.ShapeDtypeStruct((4, acts.shape[0], heads[0].shape[2] // 2), dtype),
        compiler_params=pltpu.CompilerParams(vmem_limit_bytes=12 << 20),
        cost_estimate=pl.CostEstimate(flops=1, bytes_accessed=1, transcendentals=0),
    )(*args)


def wide(value):
    return value.astype(F32) * UP if value.dtype == F16 else value.astype(F32)


def narrow(value):
    return (value * DOWN).astype(F16)


def in_hbm(value):
    return pltpu.with_memory_space_constraint(value, pltpu.HBM)


def together(*values):
    return lax.optimization_barrier(values)


def lanes(columns, rows):
    lane = lax.broadcasted_iota(jnp.int32, (rows, 128), 1)
    out = jnp.zeros((rows, 128), F32)
    for i, column in enumerate(columns):
        out = jnp.where(lane == i, column, out)
    return out


def to_all(out, columns):
    rows = columns[0].shape[0]
    square = jnp.concatenate([lanes(columns, rows), jnp.zeros((128 - rows, 128), F32)])
    out[...] = jnp.broadcast_to(square.T[None, :8], out.shape)


def square_kernel(*refs):
    values = [h[...].astype(F32) for h in refs[:-1]]
    to_all(refs[-1], [jnp.sum(h * h, axis=1, keepdims=True) for h in values])


def norm_kernel(widths, *refs):
    hidden, gains, sums, out = refs[:3], refs[3:6], refs[6], refs[7]
    total = jnp.sum(sums[...], axis=0)
    total = jnp.concatenate([total, jnp.zeros((120, 128), F32)]).T[: out.shape[0]]
    at = 0
    for i, h in enumerate(hidden):
        scale = lax.rsqrt(total[:, i : i + 1] / widths[i] + 1e-05)
        value = h[...].astype(F32) * scale * gains[i][...].astype(F32)[None]
        out[:, at : at + h.shape[1]] = value.astype(out.dtype)
        at += h.shape[1]


def join_kernel(*refs):
    at = 0
    for ref in refs[:-1]:
        refs[-1][at : at + ref.shape[0]] = ref[...]
        at += ref.shape[0]


def stats_kernel(source, home, ids, out):
    pieces, rows, width = home.shape
    row = ids[...][None].astype(F32)
    row = jnp.concatenate([row, jnp.zeros((1, 128 - rows), F32)], axis=1)
    column = jnp.broadcast_to(row, (128, 128)).T[:rows, :1]
    wanted = column.astype(jnp.int32) - source[pieces]
    top = jnp.max(home[...], axis=(0,))
    top = jnp.max(top, axis=1, keepdims=True)
    total = jnp.zeros((rows, width), F32)
    pick = jnp.zeros((rows, width), F32)
    lane = lax.broadcasted_iota(jnp.int32, (rows, width), 1)
    for i in range(pieces):
        value = home[i]
        total += jnp.exp(value - top)
        pick += jnp.where(lane == wanted - source[i] * width, value, 0.0)
    total = jnp.sum(total, axis=1, keepdims=True)
    pick = jnp.sum(pick, axis=1, keepdims=True)
    to_all(out, [top, total, pick])


def final_kernel(source, home, stats, out, picked):
    pieces, rows, width = home.shape
    tops, totals, picks = [stats[:, i, :rows] for i in range(3)]
    top = jnp.max(tops, axis=0, keepdims=True)
    logz = top + jnp.log(jnp.sum(totals * jnp.exp(tops - top), axis=0, keepdims=True))
    picked[...] = jnp.sum(picks, axis=0, keepdims=True) - logz
    square = jnp.concatenate(
        [jnp.broadcast_to(logz, (128, rows)), jnp.zeros((128, 128 - rows), F32)], axis=1
    )
    column = square.T[:rows, :1]
    for i in range(pieces):
        at = pl.multiple_of(source[i] * width, width)
        out[:, pl.ds(at, width)] = home[i] - column


def call(kernel, shapes, *args):
    def spec(v):
        small = v.dtype == jnp.int32 and v.size < 32
        return pl.BlockSpec(memory_space=pltpu.SMEM) if small else pl.BlockSpec()

    outs = [jax.ShapeDtypeStruct(s, d) for s, d in shapes]
    result = pl.pallas_call(
        kernel,
        in_specs=[spec(v) for v in args],
        out_specs=[pl.BlockSpec() for _ in outs],
        out_shape=outs,
        compiler_params=pltpu.CompilerParams(vmem_limit_bytes=16 << 20),
    )(*args)
    return result if len(outs) > 1 else result[0]


def shards(
    base_hidden,
    expert_hidden,
    anti_hidden,
    base_gain,
    expert_gain,
    anti_gain,
    base_head,
    expert_head,
    anti_head,
    strength,
    token_ids,
):
    r = lax.axis_index("rows")
    t = lax.axis_index("tensor")
    rows, c_width = token_ids.shape[0], base_head.shape[2]
    mine = lax.dynamic_slice(jnp.asarray(tables()), (r * (NY * NX) + t, 0), (1, 48))[0]
    table, source = mine[:32], mine[32:41]

    quarter = expert_head.shape[0]
    heads = []

    def swap(value, moves, *beside):
        ready = together(value, *[head for head, _ in beside])
        got = [exchange(ready[0], *move) for move in moves]
        done = [relay(h, start, quarter) for h, (_, start) in zip(ready[1:], beside)]
        results = together(*got, *done)
        heads.extend(results[len(moves) :])
        return results[: len(moves)]

    hidden = (base_hidden, expert_hidden, anti_hidden)
    gains = [in_hbm(g) for g in (base_gain, expert_gain, anti_gain)]
    width = sum(h.shape[1] for h in hidden)
    flat = [in_hbm(h) for h in hidden]
    sums = call(square_kernel, [((NY * NX, 8, 128), F32)], *flat)
    sums = lax.all_to_all(sums, "tensor", 0, 0, tiled=True)
    normed = call(
        functools.partial(norm_kernel, (D, DE, DE)), [((rows, width), BF)], *flat, *gains, sums
    )
    along_z = [("z", 0, k) for k in ALONG_Z]
    got = swap(normed, along_z, (expert_head, 0), (base_head, 0), (base_head, quarter))
    mine = jnp.concatenate([normed, *got])
    (other,) = swap(mine, [("core",)], (anti_head, 0))
    heads = heads[1:3] + [heads[0], heads[3]]
    acts = call(join_kernel, [((NZ * NC * rows, width), BF)], mine, other)

    axes = (("x", "y"), ("y", "x"))
    kept = [[], []]
    moved = [[], []]
    for i in range(4):
        for half in range(2):
            kind = BF if i < 2 else F32
            part = project(table, strength, acts, heads, 16 * half + 4 * i, half, kind)
            table, part = together(table, part)
            if i < 2:
                moved[half].append(exchange(part, axes[half][0], 0))
            else:
                kept[half].append(part)
    second_step = [
        exchange(narrow(kept[h][0] + wide(moved[h][0])), axes[h][0], 1) for h in range(2)
    ]
    sums = together(*[kept[h][1] + wide(moved[h][1]) for h in range(2)])
    sums = [sums[h] + wide(second_step[h]) for h in range(2)]
    moved = [exchange(narrow(sums[h][:2]), axes[h][1], 0) for h in range(2)]
    second_step = [
        exchange(narrow(sums[h][3] + wide(moved[h][1])), axes[h][1], 1) for h in range(2)
    ]
    logits = jnp.concatenate(
        [narrow(sums[h][2] + wide(moved[h][0]) + wide(second_step[h])) for h in range(2)], axis=1
    ).reshape(NC, NZ, rows, c_width)

    other = exchange(logits[1], "core")
    both = [jnp.stack([logits[0, i], other[i]]) for i in range(NZ)]
    home = [both[0]] + [exchange(m, *move) for m, move in zip(both[1:], along_z)]
    home = wide(jnp.concatenate(home))

    stats = call(stats_kernel, [((NY * NX, 8, 128), F32)], source, home, in_hbm(token_ids))
    stats = lax.all_to_all(stats, "tensor", 0, 0, tiled=True)
    log_probs, picked = call(
        final_kernel, [((rows, 8 * c_width), F32), ((1, rows), F32)], source, home, stats
    )
    return log_probs, picked[0]


def solution(mesh):
    return jax.shard_map(
        shards,
        mesh=mesh,
        in_specs=(
            P("rows", "tensor"),
            P("rows", "tensor"),
            P("rows", "tensor"),
            P("tensor"),
            P("tensor"),
            P("tensor"),
            P("tensor", None, "rows"),
            P("tensor", None, "rows"),
            P("tensor", None, "rows"),
            P(),
            P("rows"),
        ),
        out_specs=(P("rows", "tensor"), P("rows")),
        check_vma=False,
    )
```

```python
import functools

import jax
import jax.numpy as jnp
import numpy as np
from jax import lax
from jax.experimental import pallas as pl
from jax.experimental.pallas import tpu as pltpu
from jax.sharding import PartitionSpec as P

D = 8192
DE = 4096
VOCAB = 65536
NZ, NC, NY, NX = 4, 2, 4, 4
AXES = ("rows", "tensor")
BF = jnp.bfloat16
F16 = jnp.float16
F32 = jnp.float32
DOWN, UP = 0.0625, 16.0
ALONG_Z = (1, 3, 2)
HOME_Z = (2, 1, 3)


def device(z, c, y, x):
    return (z * NC + c) * (NY * NX) + y * NX + x


def exchange(value, axis, stage=0, by=None):
    pairs = []
    for z in range(NZ):
        for c in range(NC):
            u = by or (1 if (stage + c) % 2 == 0 else 3)
            for y in range(NY):
                for x in range(NX):
                    to = {
                        "z": (z ^ u, c, y, x),
                        "y": (z, c, y ^ u, x),
                        "x": (z, c, y, x ^ u),
                        "core": (z, 1 - c, y, x),
                    }[axis]
                    pairs.append((device(z, c, y, x), device(*to)))
    return lax.ppermute(value, AXES, pairs)


def tables():
    out = np.zeros((NZ * NC * NY * NX, 48), np.int32)
    for z in range(NZ):
        for c in range(NC):
            u, v = (1, 3) if c == 0 else (3, 1)
            first, second = (2, u, v, 0), (u, 2, 0, v)
            for y in range(NY):
                for x in range(NX):
                    row = [(y ^ j) * NX + (x ^ i) for i in first for j in second]
                    row += [(y ^ i) * NX + (x ^ j) for i in first for j in second]
                    row += [(z ^ i) * NC + k for i in (0,) + HOME_Z for k in (c, 1 - c)]
                    row += [(y * NX + x) * (VOCAB // (NY * NX))]
                    out[device(z, c, y, x), : len(row)] = row
    return out


def relay_kernel(head, out):
    out[...] = jnp.swapaxes(head[...], 0, 1)


def relay(head, start, count, step=64):
    _, n_a, c = head.shape
    return pl.pallas_call(
        relay_kernel,
        grid=(count // step,),
        in_specs=[pl.BlockSpec((step, n_a, c), lambda i: (start // step + i, 0, 0))],
        out_specs=pl.BlockSpec((n_a, step, c), lambda i: (0, i, 0)),
        out_shape=jax.ShapeDtypeStruct((n_a, count, c), head.dtype),
        compiler_params=pltpu.CompilerParams(vmem_limit_bytes=12 << 20),
        cost_estimate=pl.CostEstimate(flops=10**10, bytes_accessed=2**24, transcendentals=0),
    )(head)


def matmul_kernel(first, half, table, alpha, acts, wb0, wb1, we, wa, out):
    quarter, cols = wb0.shape[1], out.shape[2]
    for i in range(out.shape[0]):
        block = table[first + i]
        base0, base1, expert, anti = [
            jnp.dot(
                acts[:, j * quarter : (j + 1) * quarter],
                w[block, :, half * cols : (half + 1) * cols],
                preferred_element_type=F32,
            )
            for j, w in enumerate((wb0, wb1, we, wa))
        ]
        total = base0 + base1 + alpha[0] * (expert - anti)
        out[i] = total.astype(out.dtype)


def project(table, alpha, acts, heads, first, half, dtype):
    smem = pl.BlockSpec(memory_space=pltpu.SMEM)
    vmem = pl.BlockSpec(memory_space=pltpu.VMEM)
    args = (table, alpha, acts, *heads)
    return pl.pallas_call(
        functools.partial(matmul_kernel, first, half),
        in_specs=[smem] * 2 + [vmem] * (len(args) - 2),
        out_specs=vmem,
        out_shape=jax.ShapeDtypeStruct((4, acts.shape[0], heads[0].shape[2] // 2), dtype),
        compiler_params=pltpu.CompilerParams(vmem_limit_bytes=12 << 20),
        cost_estimate=pl.CostEstimate(flops=1, bytes_accessed=1, transcendentals=0),
    )(*args)


def wide(value):
    return value.astype(F32) * UP if value.dtype == F16 else value.astype(F32)


def narrow(value):
    return (value * DOWN).astype(F16)


def in_hbm(value):
    return pltpu.with_memory_space_constraint(value, pltpu.HBM)


def together(*values):
    return lax.optimization_barrier(values)


def lanes(columns, rows):
    lane = lax.broadcasted_iota(jnp.int32, (rows, 128), 1)
    out = jnp.zeros((rows, 128), F32)
    for i, column in enumerate(columns):
        out = jnp.where(lane == i, column, out)
    return out


def to_all(out, columns):
    rows = columns[0].shape[0]
    square = jnp.concatenate([lanes(columns, rows), jnp.zeros((128 - rows, 128), F32)])
    out[...] = jnp.broadcast_to(square.T[None, :8], out.shape)


def square_kernel(*refs):
    values = [h[...].astype(F32) for h in refs[:-1]]
    to_all(refs[-1], [jnp.sum(h * h, axis=1, keepdims=True) for h in values])


def norm_kernel(widths, *refs):
    hidden, gains, sums, out = refs[:3], refs[3:6], refs[6], refs[7]
    total = jnp.sum(sums[...], axis=0)
    total = jnp.concatenate([total, jnp.zeros((120, 128), F32)]).T[: out.shape[0]]
    at = 0
    for i, h in enumerate(hidden):
        scale = lax.rsqrt(total[:, i : i + 1] / widths[i] + 1e-05)
        value = h[...].astype(F32) * scale * gains[i][...].astype(F32)[None]
        out[:, at : at + h.shape[1]] = value.astype(out.dtype)
        at += h.shape[1]


def join_kernel(*refs):
    at = 0
    for ref in refs[:-1]:
        refs[-1][at : at + ref.shape[0]] = ref[...]
        at += ref.shape[0]


def stats_kernel(source, home, ids, out):
    pieces, rows, width = home.shape
    row = ids[...][None].astype(F32)
    row = jnp.concatenate([row, jnp.zeros((1, 128 - rows), F32)], axis=1)
    column = jnp.broadcast_to(row, (128, 128)).T[:rows, :1]
    wanted = column.astype(jnp.int32) - source[pieces]
    top = jnp.max(home[...], axis=(0,))
    top = jnp.max(top, axis=1, keepdims=True)
    total = jnp.zeros((rows, width), F32)
    pick = jnp.zeros((rows, width), F32)
    lane = lax.broadcasted_iota(jnp.int32, (rows, width), 1)
    for i in range(pieces):
        value = home[i]
        total += jnp.exp(value - top)
        pick += jnp.where(lane == wanted - source[i] * width, value, 0.0)
    total = jnp.sum(total, axis=1, keepdims=True)
    pick = jnp.sum(pick, axis=1, keepdims=True)
    to_all(out, [top, total, pick])


def final_kernel(source, home, stats, out, picked):
    pieces, rows, width = home.shape
    tops, totals, picks = [stats[:, i, :rows] for i in range(3)]
    top = jnp.max(tops, axis=0, keepdims=True)
    logz = top + jnp.log(jnp.sum(totals * jnp.exp(tops - top), axis=0, keepdims=True))
    picked[...] = jnp.sum(picks, axis=0, keepdims=True) - logz
    square = jnp.concatenate(
        [jnp.broadcast_to(logz, (128, rows)), jnp.zeros((128, 128 - rows), F32)], axis=1
    )
    column = square.T[:rows, :1]
    for i in range(pieces):
        at = pl.multiple_of(source[i] * width, width)
        out[:, pl.ds(at, width)] = home[i] - column


def call(kernel, shapes, *args):
    def spec(v):
        small = v.dtype == jnp.int32 and v.size < 32
        return pl.BlockSpec(memory_space=pltpu.SMEM) if small else pl.BlockSpec()

    outs = [jax.ShapeDtypeStruct(s, d) for s, d in shapes]
    result = pl.pallas_call(
        kernel,
        in_specs=[spec(v) for v in args],
        out_specs=[pl.BlockSpec() for _ in outs],
        out_shape=outs,
        compiler_params=pltpu.CompilerParams(vmem_limit_bytes=16 << 20),
    )(*args)
    return result if len(outs) > 1 else result[0]


def shards(
    base_hidden,
    expert_hidden,
    anti_hidden,
    base_gain,
    expert_gain,
    anti_gain,
    base_head,
    expert_head,
    anti_head,
    strength,
    token_ids,
):
    r = lax.axis_index("rows")
    t = lax.axis_index("tensor")
    rows, c_width = token_ids.shape[0], base_head.shape[2]
    mine = lax.dynamic_slice(jnp.asarray(tables()), (r * (NY * NX) + t, 0), (1, 48))[0]
    table, source = mine[:32], mine[32:41]

    quarter = expert_head.shape[0]
    heads = []

    def swap(value, moves, *beside):
        ready = together(value, *[head for head, _ in beside])
        got = [exchange(ready[0], *move) for move in moves]
        done = [relay(h, start, quarter) for h, (_, start) in zip(ready[1:], beside)]
        results = together(*got, *done)
        heads.extend(results[len(moves) :])
        return results[: len(moves)]

    hidden = (base_hidden, expert_hidden, anti_hidden)
    gains = [in_hbm(g) for g in (base_gain, expert_gain, anti_gain)]
    width = sum(h.shape[1] for h in hidden)
    flat = [in_hbm(h) for h in hidden]
    sums = call(square_kernel, [((NY * NX, 8, 128), F32)], *flat)
    sums = lax.all_to_all(sums, "tensor", 0, 0, tiled=True)
    normed = call(
        functools.partial(norm_kernel, (D, DE, DE)), [((rows, width), BF)], *flat, *gains, sums
    )
    along_z = [("z", 0, k) for k in ALONG_Z]
    got = swap(normed, along_z, (expert_head, 0), (base_head, 0), (base_head, quarter))
    mine = jnp.concatenate([normed, *got])
    (other,) = swap(mine, [("core",)], (anti_head, 0))
    heads = heads[1:3] + [heads[0], heads[3]]
    acts = call(join_kernel, [((NZ * NC * rows, width), BF)], mine, other)

    axes = (("x", "y"), ("y", "x"))
    kept = [[], []]
    moved = [[], []]
    for i in range(4):
        for half in range(2):
            kind = BF if i < 2 else F32
            part = project(table, strength, acts, heads, 16 * half + 4 * i, half, kind)
            table, part = together(table, part)
            if i < 2:
                moved[half].append(exchange(part, axes[half][0], 0))
            else:
                kept[half].append(part)
    second_step = [
        exchange(narrow(kept[h][0] + wide(moved[h][0])), axes[h][0], 1) for h in range(2)
    ]
    sums = together(*[kept[h][1] + wide(moved[h][1]) for h in range(2)])
    sums = [sums[h] + wide(second_step[h]) for h in range(2)]
    moved = [
        [exchange(narrow(sums[h][i]), axes[h][1], 0) for i in (1, 0)] for h in range(2)
    ]
    second_step = [
        exchange(narrow(sums[h][3] + wide(moved[h][0])), axes[h][1], 1) for h in range(2)
    ]
    logits = jnp.concatenate(
        [narrow(sums[h][2] + wide(moved[h][1]) + wide(second_step[h])) for h in range(2)], axis=1
    ).reshape(NC, NZ, rows, c_width)

    other = exchange(logits[1], "core")
    home = [jnp.stack([logits[0, 0], other[0]])]
    for k in HOME_Z:
        i = 1 + ALONG_Z.index(k)
        home.append(exchange(jnp.stack([logits[0, i], other[i]]), "z", by=k))
    home = wide(jnp.concatenate(home))

    stats = call(stats_kernel, [((NY * NX, 8, 128), F32)], source, home, in_hbm(token_ids))
    stats = lax.all_to_all(stats, "tensor", 0, 0, tiled=True)
    log_probs, picked = call(
        final_kernel, [((rows, 8 * c_width), F32), ((1, rows), F32)], source, home, stats
    )
    return log_probs, picked[0]


def solution(mesh):
    return jax.shard_map(
        shards,
        mesh=mesh,
        in_specs=(
            P("rows", "tensor"),
            P("rows", "tensor"),
            P("rows", "tensor"),
            P("tensor"),
            P("tensor"),
            P("tensor"),
            P("tensor", None, "rows"),
            P("tensor", None, "rows"),
            P("tensor", None, "rows"),
            P(),
            P("rows"),
        ),
        out_specs=(P("rows", "tensor"), P("rows")),
        check_vma=False,
    )
```

```python
import functools

import jax
import jax.numpy as jnp
import numpy as np
from jax import lax
from jax.experimental import pallas as pl
from jax.experimental.pallas import tpu as pltpu
from jax.sharding import PartitionSpec as P

D = 8192
DE = 4096
VOCAB = 65536
NZ, NC, NY, NX = 4, 2, 4, 4
AXES = ("rows", "tensor")
BF = jnp.bfloat16
F16 = jnp.float16
F32 = jnp.float32
DOWN, UP = 0.0625, 16.0
LONG = pl.CostEstimate(flops=10**10, bytes_accessed=2**24, transcendentals=0)
ALONG_Z = (1, 3, 2)
HOME_Z = (2, 1, 3)


def device(z, c, y, x):
    return (z * NC + c) * (NY * NX) + y * NX + x


def exchange(value, axis, stage=0, by=None):
    pairs = []
    for z in range(NZ):
        for c in range(NC):
            u = by or (1 if (stage + c) % 2 == 0 else 3)
            for y in range(NY):
                for x in range(NX):
                    to = {
                        "z": (z ^ u, c, y, x),
                        "y": (z, c, y ^ u, x),
                        "x": (z, c, y, x ^ u),
                        "core": (z, 1 - c, y, x),
                    }[axis]
                    pairs.append((device(z, c, y, x), device(*to)))
    return lax.ppermute(value, AXES, pairs)


def tables():
    out = np.zeros((NZ * NC * NY * NX, 48), np.int32)
    for z in range(NZ):
        for c in range(NC):
            u, v = (1, 3) if c == 0 else (3, 1)
            first, second = (2, u, v, 0), (u, 2, 0, v)
            for y in range(NY):
                for x in range(NX):
                    row = [(y ^ j) * NX + (x ^ i) for i in first for j in second]
                    row += [(y ^ i) * NX + (x ^ j) for i in first for j in second]
                    row += [(z ^ i) * NC + k for i in (0,) + HOME_Z for k in (c, 1 - c)]
                    row += [(y * NX + x) * (VOCAB // (NY * NX))]
                    out[device(z, c, y, x), : len(row)] = row
    return out


def relay_kernel(head, out):
    out[...] = jnp.swapaxes(head[...], 0, 1)


def relay(head, start, count, step=64):
    _, n_a, c = head.shape
    return pl.pallas_call(
        relay_kernel,
        grid=(count // step,),
        in_specs=[pl.BlockSpec((step, n_a, c), lambda i: (start // step + i, 0, 0))],
        out_specs=pl.BlockSpec((n_a, step, c), lambda i: (0, i, 0)),
        out_shape=jax.ShapeDtypeStruct((n_a, count, c), head.dtype),
        compiler_params=pltpu.CompilerParams(vmem_limit_bytes=12 << 20),
        cost_estimate=LONG,
    )(head)


def matmul_kernel(first, half, table, alpha, acts, wb0, wb1, we, wa, out):
    quarter, cols = wb0.shape[1], out.shape[2]
    for i in range(out.shape[0]):
        block = table[first + i]
        base0, base1, expert, anti = [
            jnp.dot(
                acts[:, j * quarter : (j + 1) * quarter],
                w[block, :, half * cols : (half + 1) * cols],
                preferred_element_type=F32,
            )
            for j, w in enumerate((wb0, wb1, we, wa))
        ]
        total = base0 + base1 + alpha[0] * (expert - anti)
        out[i] = total.astype(out.dtype)


def project(table, alpha, acts, heads, first, half, dtype):
    smem = pl.BlockSpec(memory_space=pltpu.SMEM)
    vmem = pl.BlockSpec(memory_space=pltpu.VMEM)
    args = (table, alpha, acts, *heads)
    return pl.pallas_call(
        functools.partial(matmul_kernel, first, half),
        in_specs=[smem] * 2 + [vmem] * (len(args) - 2),
        out_specs=vmem,
        out_shape=jax.ShapeDtypeStruct((4, acts.shape[0], heads[0].shape[2] // 2), dtype),
        compiler_params=pltpu.CompilerParams(vmem_limit_bytes=12 << 20),
        cost_estimate=pl.CostEstimate(flops=1, bytes_accessed=1, transcendentals=0),
    )(*args)


def wide(value):
    return value.astype(F32) * UP if value.dtype == F16 else value.astype(F32)


def narrow(value):
    return (value * DOWN).astype(F16)


def in_hbm(value):
    return pltpu.with_memory_space_constraint(value, pltpu.HBM)


def together(*values):
    return lax.optimization_barrier(values)


def lanes(columns, rows):
    lane = lax.broadcasted_iota(jnp.int32, (rows, 128), 1)
    out = jnp.zeros((rows, 128), F32)
    for i, column in enumerate(columns):
        out = jnp.where(lane == i, column, out)
    return out


def to_all(out, columns):
    rows = columns[0].shape[0]
    square = jnp.concatenate([lanes(columns, rows), jnp.zeros((128 - rows, 128), F32)])
    out[...] = jnp.broadcast_to(square.T[None, :8], out.shape)


def square_kernel(*refs):
    values = [h[...].astype(F32) for h in refs[:-1]]
    to_all(refs[-1], [jnp.sum(h * h, axis=1, keepdims=True) for h in values])


def norm_kernel(widths, *refs):
    hidden, gains, sums, out = refs[:3], refs[3:6], refs[6], refs[7]
    total = jnp.sum(sums[...], axis=0)
    total = jnp.concatenate([total, jnp.zeros((120, 128), F32)]).T[: out.shape[0]]
    at = 0
    for i, h in enumerate(hidden):
        scale = lax.rsqrt(total[:, i : i + 1] / widths[i] + 1e-05)
        value = h[...].astype(F32) * scale * gains[i][...].astype(F32)[None]
        out[:, at : at + h.shape[1]] = value.astype(out.dtype)
        at += h.shape[1]


def join_kernel(*refs):
    at = 0
    for ref in refs[:-1]:
        refs[-1][at : at + ref.shape[0]] = ref[...]
        at += ref.shape[0]


def stats_kernel(source, home, ids, out):
    pieces, rows, width = home.shape
    row = ids[...][None].astype(F32)
    row = jnp.concatenate([row, jnp.zeros((1, 128 - rows), F32)], axis=1)
    column = jnp.broadcast_to(row, (128, 128)).T[:rows, :1]
    wanted = column.astype(jnp.int32) - source[pieces]
    top = jnp.max(home[...], axis=(0,))
    top = jnp.max(top, axis=1, keepdims=True)
    total = jnp.zeros((rows, width), F32)
    pick = jnp.zeros((rows, width), F32)
    lane = lax.broadcasted_iota(jnp.int32, (rows, width), 1)
    for i in range(pieces):
        value = home[i]
        total += jnp.exp(value - top)
        pick += jnp.where(lane == wanted - source[i] * width, value, 0.0)
    total = jnp.sum(total, axis=1, keepdims=True)
    pick = jnp.sum(pick, axis=1, keepdims=True)
    to_all(out, [top, total, pick])


def final_kernel(source, home, stats, out, picked):
    pieces, rows, width = home.shape
    tops, totals, picks = [stats[:, i, :rows] for i in range(3)]
    top = jnp.max(tops, axis=0, keepdims=True)
    logz = top + jnp.log(jnp.sum(totals * jnp.exp(tops - top), axis=0, keepdims=True))
    picked[...] = jnp.sum(picks, axis=0, keepdims=True) - logz
    square = jnp.concatenate(
        [jnp.broadcast_to(logz, (128, rows)), jnp.zeros((128, 128 - rows), F32)], axis=1
    )
    column = square.T[:rows, :1]
    for i in range(pieces):
        at = pl.multiple_of(source[i] * width, width)
        out[:, pl.ds(at, width)] = home[i] - column


def call(kernel, shapes, *args, cost=None):
    def spec(v):
        small = v.dtype == jnp.int32 and v.size < 32
        return pl.BlockSpec(memory_space=pltpu.SMEM) if small else pl.BlockSpec()

    outs = [jax.ShapeDtypeStruct(s, d) for s, d in shapes]
    result = pl.pallas_call(
        kernel,
        in_specs=[spec(v) for v in args],
        out_specs=[pl.BlockSpec() for _ in outs],
        out_shape=outs,
        compiler_params=pltpu.CompilerParams(vmem_limit_bytes=16 << 20),
        cost_estimate=cost,
    )(*args)
    return result if len(outs) > 1 else result[0]


def shards(
    base_hidden,
    expert_hidden,
    anti_hidden,
    base_gain,
    expert_gain,
    anti_gain,
    base_head,
    expert_head,
    anti_head,
    strength,
    token_ids,
):
    r = lax.axis_index("rows")
    t = lax.axis_index("tensor")
    rows, c_width = token_ids.shape[0], base_head.shape[2]
    mine = lax.dynamic_slice(jnp.asarray(tables()), (r * (NY * NX) + t, 0), (1, 48))[0]
    table, source = mine[:32], mine[32:41]

    quarter = expert_head.shape[0]
    heads = []

    def swap(value, moves, *beside):
        ready = together(value, *[head for head, _ in beside])
        got = [exchange(ready[0], *move) for move in moves]
        done = [relay(h, start, quarter) for h, (_, start) in zip(ready[1:], beside)]
        results = together(*got, *done)
        heads.extend(results[len(moves) :])
        return results[: len(moves)]

    hidden = (base_hidden, expert_hidden, anti_hidden)
    gains = [in_hbm(g) for g in (base_gain, expert_gain, anti_gain)]
    width = sum(h.shape[1] for h in hidden)
    flat = [in_hbm(h) for h in hidden]
    sums = call(square_kernel, [((NY * NX, 8, 128), F32)], *flat)
    sums = lax.all_to_all(sums, "tensor", 0, 0, tiled=True)
    normed = call(
        functools.partial(norm_kernel, (D, DE, DE)),
        [((rows, width), BF)],
        *flat,
        *gains,
        sums,
        cost=LONG,
    )
    along_z = [("z", 0, k) for k in ALONG_Z]
    got = swap(normed, along_z, (base_head, 0), (base_head, quarter), (expert_head, 0))
    mine = jnp.concatenate([normed, *got])
    (other,) = swap(mine, [("core",)], (anti_head, 0))
    acts = call(join_kernel, [((NZ * NC * rows, width), BF)], mine, other)

    axes = (("x", "y"), ("y", "x"))
    kept = [[], []]
    moved = [[], []]
    second_step = []
    for i in range(4):
        for half in range(2):
            kind = BF if i < 2 else F32
            part = project(table, strength, acts, heads, 16 * half + 4 * i, half, kind)
            table, part = together(table, part)
            if i < 2:
                moved[half].append(exchange(part, axes[half][0], 0))
            else:
                kept[half].append(part)
        if i == 2:
            totals = [narrow(kept[h][0] + wide(moved[h][0])) for h in range(2)]
            second_step = [exchange(totals[h], axes[h][0], 1) for h in range(2)]
            table, _ = together(table, totals[1])
    own = together(kept[0][1], kept[1][1])
    sums = together(*[own[h] + wide(moved[h][1]) for h in range(2)])
    sums = [sums[h] + wide(second_step[h]) for h in range(2)]
    moved = [
        [exchange(narrow(sums[h][i]), axes[h][1], 0) for i in (1, 0)] for h in range(2)
    ]
    second_step = [
        exchange(narrow(sums[h][3] + wide(moved[h][0])), axes[h][1], 1) for h in range(2)
    ]
    logits = jnp.concatenate(
        [narrow(sums[h][2] + wide(moved[h][1]) + wide(second_step[h])) for h in range(2)], axis=1
    ).reshape(NC, NZ, rows, c_width)

    other = exchange(logits[1], "core")
    home = [jnp.stack([logits[0, 0], other[0]])]
    for k in HOME_Z:
        i = 1 + ALONG_Z.index(k)
        home.append(exchange(jnp.stack([logits[0, i], other[i]]), "z", by=k))
    home = wide(jnp.concatenate(home))

    stats = call(stats_kernel, [((NY * NX, 8, 128), F32)], source, home, in_hbm(token_ids))
    stats = lax.all_to_all(stats, "tensor", 0, 0, tiled=True)
    log_probs, picked = call(
        final_kernel, [((rows, 8 * c_width), F32), ((1, rows), F32)], source, home, stats
    )
    return log_probs, picked[0]


def solution(mesh):
    return jax.shard_map(
        shards,
        mesh=mesh,
        in_specs=(
            P("rows", "tensor"),
            P("rows", "tensor"),
            P("rows", "tensor"),
            P("tensor"),
            P("tensor"),
            P("tensor"),
            P("tensor", None, "rows"),
            P("tensor", None, "rows"),
            P("tensor", None, "rows"),
            P(),
            P("rows"),
        ),
        out_specs=(P("rows", "tensor"), P("rows")),
        check_vma=False,
    )
```

```python
import functools

import jax
import jax.numpy as jnp
from jax import lax
from jax.experimental import pallas as pl
from jax.experimental.pallas import tpu as pltpu
from jax.sharding import PartitionSpec as P

D = 8192
DE = 4096
VOCAB = 65536
NZ, NC, NY, NX = 4, 2, 4, 4
AXES = ("rows", "tensor")
BF = jnp.bfloat16
F16 = jnp.float16
F32 = jnp.float32
DOWN, UP = 0.0625, 16.0
LONG = pl.CostEstimate(flops=10**10, bytes_accessed=2**24, transcendentals=0)
ALONG_Z = (1, 3, 2)
HOME_Z = (2, 1, 3)


def device(z, c, y, x):
    return (z * NC + c) * (NY * NX) + y * NX + x


def exchange(value, axis, stage=0, by=None):
    pairs = []
    for z in range(NZ):
        for c in range(NC):
            u = by or (1 if (stage + c) % 2 == 0 else 3)
            for y in range(NY):
                for x in range(NX):
                    to = {
                        "z": (z ^ u, c, y, x),
                        "y": (z, c, y ^ u, x),
                        "x": (z, c, y, x ^ u),
                        "core": (z, 1 - c, y, x),
                    }[axis]
                    pairs.append((device(z, c, y, x), device(*to)))
    return lax.ppermute(value, AXES, pairs)


def here():
    r, t = lax.axis_index("rows"), lax.axis_index("tensor")
    return r // NC, r % NC, t // NX, t % NX


def sources():
    z, c, _, _ = here()
    return [(z ^ k) * NC + core for k in (0,) + HOME_Z for core in (c, 1 - c)]


def relay_kernel(head, out):
    out[...] = jnp.swapaxes(head[...], 0, 1)


def relay(head, start, count, step=64):
    _, n_a, c = head.shape
    return pl.pallas_call(
        relay_kernel,
        grid=(count // step,),
        in_specs=[pl.BlockSpec((step, n_a, c), lambda i: (start // step + i, 0, 0))],
        out_specs=pl.BlockSpec((n_a, step, c), lambda i: (0, i, 0)),
        out_shape=jax.ShapeDtypeStruct((n_a, count, c), head.dtype),
        compiler_params=pltpu.CompilerParams(vmem_limit_bytes=12 << 20),
        cost_estimate=pl.CostEstimate(flops=0, bytes_accessed=2**23, transcendentals=0),
    )(head)


def matmul_kernel(step, half, alpha, acts, wb0, wb1, we, wa, out):
    quarter, cols = wb0.shape[1], out.shape[2]
    _, c, y, x = here()
    u, v = 1 + 2 * c, 3 - 2 * c
    first, second = (2, u, v, 0)[step], (u, 2, 0, v)
    for i in range(out.shape[0]):
        along_y, along_x = (second[i], first) if half == 0 else (first, second[i])
        block = (y ^ along_y) * NX + (x ^ along_x)
        base0, base1, expert, anti = [
            jnp.dot(
                acts[:, j * quarter : (j + 1) * quarter],
                w[block, :, half * cols : (half + 1) * cols],
                preferred_element_type=F32,
            )
            for j, w in enumerate((wb0, wb1, we, wa))
        ]
        total = base0 + base1 + alpha[0] * (expert - anti)
        out[i] = total.astype(out.dtype)


def project(alpha, acts, heads, step, half, dtype):
    smem = pl.BlockSpec(memory_space=pltpu.SMEM)
    vmem = pl.BlockSpec(memory_space=pltpu.VMEM)
    return pl.pallas_call(
        functools.partial(matmul_kernel, step, half),
        in_specs=[smem] + [vmem] * (1 + len(heads)),
        out_specs=vmem,
        out_shape=jax.ShapeDtypeStruct((4, acts.shape[0], heads[0].shape[2] // 2), dtype),
        compiler_params=pltpu.CompilerParams(vmem_limit_bytes=12 << 20),
        cost_estimate=pl.CostEstimate(flops=1, bytes_accessed=1, transcendentals=0),
    )(alpha, acts, *heads)


def wide(value):
    return value.astype(F32) * UP if value.dtype == F16 else value.astype(F32)


def narrow(value):
    return (value * DOWN).astype(F16)


def in_hbm(value):
    return pltpu.with_memory_space_constraint(value, pltpu.HBM)


def together(*values):
    return lax.optimization_barrier(values)


def lanes(columns, rows):
    lane = lax.broadcasted_iota(jnp.int32, (rows, 128), 1)
    out = jnp.zeros((rows, 128), F32)
    for i, column in enumerate(columns):
        out = jnp.where(lane == i, column, out)
    return out


def to_all(out, columns):
    rows = columns[0].shape[0]
    square = jnp.concatenate([lanes(columns, rows), jnp.zeros((128 - rows, 128), F32)])
    out[...] = jnp.broadcast_to(square.T[None, :8], out.shape)


def square_kernel(*refs):
    values = [h[...].astype(F32) for h in refs[:-1]]
    to_all(refs[-1], [jnp.sum(h * h, axis=1, keepdims=True) for h in values])


def norm_kernel(widths, *refs):
    hidden, gains, sums, out = refs[:3], refs[3:6], refs[6], refs[7]
    total = jnp.sum(sums[...], axis=0)
    total = jnp.concatenate([total, jnp.zeros((120, 128), F32)]).T[: out.shape[0]]
    at = 0
    for i, h in enumerate(hidden):
        scale = lax.rsqrt(total[:, i : i + 1] / widths[i] + 1e-05)
        value = h[...].astype(F32) * scale * gains[i][...].astype(F32)[None]
        out[:, at : at + h.shape[1]] = value.astype(out.dtype)
        at += h.shape[1]


def join_kernel(*refs):
    at = 0
    for ref in refs[:-1]:
        refs[-1][at : at + ref.shape[0]] = ref[...]
        at += ref.shape[0]


def stats_kernel(home, ids, out):
    pieces, rows, width = home.shape
    source = sources()
    row = ids[...][None].astype(F32)
    row = jnp.concatenate([row, jnp.zeros((1, 128 - rows), F32)], axis=1)
    column = jnp.broadcast_to(row, (128, 128)).T[:rows, :1]
    wanted = column.astype(jnp.int32) - lax.axis_index("tensor") * (VOCAB // (NY * NX))
    top = jnp.max(home[...], axis=(0,))
    top = jnp.max(top, axis=1, keepdims=True)
    total = jnp.zeros((rows, width), F32)
    pick = jnp.zeros((rows, width), F32)
    lane = lax.broadcasted_iota(jnp.int32, (rows, width), 1)
    for i in range(pieces):
        value = home[i]
        total += jnp.exp(value - top)
        pick += jnp.where(lane == wanted - source[i] * width, value, 0.0)
    total = jnp.sum(total, axis=1, keepdims=True)
    pick = jnp.sum(pick, axis=1, keepdims=True)
    to_all(out, [top, total, pick])


def final_kernel(home, stats, out, picked):
    pieces, rows, width = home.shape
    source = sources()
    tops, totals, picks = [stats[:, i, :rows] for i in range(3)]
    top = jnp.max(tops, axis=0, keepdims=True)
    logz = top + jnp.log(jnp.sum(totals * jnp.exp(tops - top), axis=0, keepdims=True))
    picked[...] = jnp.sum(picks, axis=0, keepdims=True) - logz
    square = jnp.concatenate(
        [jnp.broadcast_to(logz, (128, rows)), jnp.zeros((128, 128 - rows), F32)], axis=1
    )
    column = square.T[:rows, :1]
    for i in range(pieces):
        at = pl.multiple_of(source[i] * width, width)
        out[:, pl.ds(at, width)] = home[i] - column


def call(kernel, shapes, *args, cost=None):
    outs = [jax.ShapeDtypeStruct(s, d) for s, d in shapes]
    result = pl.pallas_call(
        kernel,
        in_specs=[pl.BlockSpec() for _ in args],
        out_specs=[pl.BlockSpec() for _ in outs],
        out_shape=outs,
        compiler_params=pltpu.CompilerParams(vmem_limit_bytes=16 << 20),
        cost_estimate=cost,
    )(*args)
    return result if len(outs) > 1 else result[0]


def shards(
    base_hidden,
    expert_hidden,
    anti_hidden,
    base_gain,
    expert_gain,
    anti_gain,
    base_head,
    expert_head,
    anti_head,
    strength,
    token_ids,
):
    rows, c_width = token_ids.shape[0], base_head.shape[2]

    quarter = expert_head.shape[0]
    heads = []

    def swap(value, moves, *beside):
        ready = together(value, *[head for head, _ in beside])
        got = [exchange(ready[0], *move) for move in moves]
        done = [relay(h, start, quarter) for h, (_, start) in zip(ready[1:], beside)]
        results = together(*got, *done)
        heads.extend(results[len(moves) :])
        return results[: len(moves)]

    hidden = (base_hidden, expert_hidden, anti_hidden)
    gains = [in_hbm(g) for g in (base_gain, expert_gain, anti_gain)]
    width = sum(h.shape[1] for h in hidden)
    flat = [in_hbm(h) for h in hidden]
    sums = call(square_kernel, [((NY * NX, 8, 128), F32)], *flat)
    sums = lax.all_to_all(sums, "tensor", 0, 0, tiled=True)
    normed = call(
        functools.partial(norm_kernel, (D, DE, DE)),
        [((rows, width), BF)],
        *flat,
        *gains,
        sums,
        cost=LONG,
    )
    strength, normed = together(strength, normed)
    along_z = [("z", 0, k) for k in ALONG_Z]
    got = swap(normed, along_z, (base_head, 0), (base_head, quarter), (expert_head, 0))
    mine = jnp.concatenate([normed, *got])
    (other,) = swap(mine, [("core",)], (anti_head, 0))
    acts = call(join_kernel, [((NZ * NC * rows, width), BF)], mine, other)

    axes = (("x", "y"), ("y", "x"))
    kept = [[], []]
    moved = [[], []]
    second_step = []
    for i in range(4):
        for half in range(2):
            kind = BF if i < 2 else F32
            part = project(strength, acts, heads, i, half, kind)
            strength, part = together(strength, part)
            if i < 2:
                moved[half].append(exchange(part, axes[half][0], 0))
            else:
                kept[half].append(part)
        if i == 2:
            totals = [narrow(kept[h][0] + wide(moved[h][0])) for h in range(2)]
            second_step = [exchange(totals[h], axes[h][0], 1) for h in range(2)]
            strength, _ = together(strength, totals[1])
    own = together(kept[0][1], kept[1][1])
    sums = together(*[own[h] + wide(moved[h][1]) for h in range(2)])
    sums = [sums[h] + wide(second_step[h]) for h in range(2)]
    moved = [
        [exchange(narrow(sums[h][i]), axes[h][1], 0) for i in (1, 0)] for h in range(2)
    ]
    second_step = [
        exchange(narrow(sums[h][3] + wide(moved[h][0])), axes[h][1], 1) for h in range(2)
    ]
    logits = jnp.concatenate(
        [narrow(sums[h][2] + wide(moved[h][1]) + wide(second_step[h])) for h in range(2)], axis=1
    ).reshape(NC, NZ, rows, c_width)

    other = exchange(logits[1], "core")
    home = [jnp.stack([logits[0, 0], other[0]])]
    for k in HOME_Z:
        i = 1 + ALONG_Z.index(k)
        home.append(exchange(jnp.stack([logits[0, i], other[i]]), "z", by=k))
    home = wide(jnp.concatenate(home))

    stats = call(stats_kernel, [((NY * NX, 8, 128), F32)], home, in_hbm(token_ids))
    stats = lax.all_to_all(stats, "tensor", 0, 0, tiled=True)
    log_probs, picked = call(
        final_kernel, [((rows, 8 * c_width), F32), ((1, rows), F32)], home, stats
    )
    return log_probs, picked[0]


def solution(mesh):
    return jax.shard_map(
        shards,
        mesh=mesh,
        in_specs=(
            P("rows", "tensor"),
            P("rows", "tensor"),
            P("rows", "tensor"),
            P("tensor"),
            P("tensor"),
            P("tensor"),
            P("tensor", None, "rows"),
            P("tensor", None, "rows"),
            P("tensor", None, "rows"),
            P(),
            P("rows"),
        ),
        out_specs=(P("rows", "tensor"), P("rows")),
        check_vma=False,
    )
```

```python
import functools

import jax
import jax.numpy as jnp
from jax import lax
from jax.experimental import pallas as pl
from jax.experimental.pallas import tpu as pltpu
from jax.sharding import PartitionSpec as P

D = 8192
DE = 4096
VOCAB = 65536
NZ, NC, NY, NX = 4, 2, 4, 4
AXES = ("rows", "tensor")
BF = jnp.bfloat16
F16 = jnp.float16
F32 = jnp.float32
DOWN, UP = 0.0625, 16.0
LONG = pl.CostEstimate(flops=10**10, bytes_accessed=2**24, transcendentals=0)
ALONG_Z = (1, 3, 2)
HOME_Z = (2, 1, 3)


def device(z, c, y, x):
    return (z * NC + c) * (NY * NX) + y * NX + x


def exchange(value, axis, stage=0, by=None):
    pairs = []
    for z in range(NZ):
        for c in range(NC):
            u = by or (1 if (stage + c) % 2 == 0 else 3)
            for y in range(NY):
                for x in range(NX):
                    to = {
                        "z": (z ^ u, c, y, x),
                        "y": (z, c, y ^ u, x),
                        "x": (z, c, y, x ^ u),
                        "core": (z, 1 - c, y, x),
                    }[axis]
                    pairs.append((device(z, c, y, x), device(*to)))
    return lax.ppermute(value, AXES, pairs)


def here():
    r, t = lax.axis_index("rows"), lax.axis_index("tensor")
    return r // NC, r % NC, t // NX, t % NX


def sources():
    z, c, _, _ = here()
    return [(z ^ k) * NC + core for k in (0,) + HOME_Z for core in (c, 1 - c)]


def relay_kernel(head, out):
    out[...] = jnp.swapaxes(head[...], 0, 1)


def relay(head, start, count, step=64):
    _, n_a, c = head.shape
    return pl.pallas_call(
        relay_kernel,
        grid=(count // step,),
        in_specs=[pl.BlockSpec((step, n_a, c), lambda i: (start // step + i, 0, 0))],
        out_specs=pl.BlockSpec((n_a, step, c), lambda i: (0, i, 0)),
        out_shape=jax.ShapeDtypeStruct((n_a, count, c), head.dtype),
        compiler_params=pltpu.CompilerParams(vmem_limit_bytes=12 << 20),
        cost_estimate=pl.CostEstimate(flops=0, bytes_accessed=2**23, transcendentals=0),
    )(head)


def matmul_kernel(step, half, alpha, acts, wb0, wb1, we, wa, out):
    quarter, cols = wb0.shape[1], out.shape[2]
    _, c, y, x = here()
    u, v = 1 + 2 * c, 3 - 2 * c
    first, second = (2, u, v, 0)[step], (u, 2, 0, v)
    for i in range(out.shape[0]):
        along_y, along_x = (second[i], first) if half == 0 else (first, second[i])
        block = (y ^ along_y) * NX + (x ^ along_x)
        base0, base1, expert, anti = [
            jnp.dot(
                acts[:, j * quarter : (j + 1) * quarter],
                w[block, :, half * cols : (half + 1) * cols],
                preferred_element_type=F32,
            )
            for j, w in enumerate((wb0, wb1, we, wa))
        ]
        total = base0 + base1 + alpha[0] * (expert - anti)
        out[i] = total.astype(out.dtype)


def project(alpha, acts, heads, step, half, dtype):
    smem = pl.BlockSpec(memory_space=pltpu.SMEM)
    vmem = pl.BlockSpec(memory_space=pltpu.VMEM)
    return pl.pallas_call(
        functools.partial(matmul_kernel, step, half),
        in_specs=[smem] + [vmem] * (1 + len(heads)),
        out_specs=vmem,
        out_shape=jax.ShapeDtypeStruct((4, acts.shape[0], heads[0].shape[2] // 2), dtype),
        compiler_params=pltpu.CompilerParams(vmem_limit_bytes=12 << 20),
        cost_estimate=pl.CostEstimate(flops=1, bytes_accessed=1, transcendentals=0),
    )(alpha, acts, *heads)


def wide(value):
    return value.astype(F32) * UP if value.dtype == F16 else value.astype(F32)


def narrow(value):
    return (value * DOWN).astype(F16)


def in_hbm(value):
    return pltpu.with_memory_space_constraint(value, pltpu.HBM)


def together(*values):
    return lax.optimization_barrier(values)


def lanes(columns, rows):
    lane = lax.broadcasted_iota(jnp.int32, (rows, 128), 1)
    out = jnp.zeros((rows, 128), F32)
    for i, column in enumerate(columns):
        out = jnp.where(lane == i, column, out)
    return out


def to_all(out, columns):
    rows = columns[0].shape[0]
    square = jnp.concatenate([lanes(columns, rows), jnp.zeros((128 - rows, 128), F32)])
    out[...] = jnp.broadcast_to(square.T[None, :8], out.shape)


def square_kernel(*refs):
    values = [h[...].astype(F32) for h in refs[:-1]]
    to_all(refs[-1], [jnp.sum(h * h, axis=1, keepdims=True) for h in values])


def norm_kernel(widths, *refs):
    hidden, gains, sums, out = refs[:3], refs[3:6], refs[6], refs[7]
    total = jnp.sum(sums[...], axis=0)
    total = jnp.concatenate([total, jnp.zeros((120, 128), F32)]).T[: out.shape[0]]
    at = 0
    for i, h in enumerate(hidden):
        scale = lax.rsqrt(total[:, i : i + 1] / widths[i] + 1e-05)
        value = h[...].astype(F32) * scale * gains[i][...].astype(F32)[None]
        out[:, at : at + h.shape[1]] = value.astype(out.dtype)
        at += h.shape[1]


def join_kernel(*refs):
    at = 0
    for ref in refs[:-1]:
        refs[-1][at : at + ref.shape[0]] = ref[...]
        at += ref.shape[0]


def stats_kernel(home, ids, out):
    pieces, rows, width = home.shape
    source = sources()
    row = ids[...][None].astype(F32)
    row = jnp.concatenate([row, jnp.zeros((1, 128 - rows), F32)], axis=1)
    column = jnp.broadcast_to(row, (128, 128)).T[:rows, :1]
    wanted = column.astype(jnp.int32) - lax.axis_index("tensor") * (VOCAB // (NY * NX))
    top = jnp.max(home[...], axis=(0,))
    top = jnp.max(top, axis=1, keepdims=True)
    total = jnp.zeros((rows, width), F32)
    pick = jnp.zeros((rows, width), F32)
    lane = lax.broadcasted_iota(jnp.int32, (rows, width), 1)
    for i in range(pieces):
        value = home[i]
        total += jnp.exp(value - top)
        pick += jnp.where(lane == wanted - source[i] * width, value, 0.0)
    total = jnp.sum(total, axis=1, keepdims=True)
    pick = jnp.sum(pick, axis=1, keepdims=True)
    to_all(out, [top, total, pick])


def final_kernel(home, stats, out, picked):
    pieces, rows, width = home.shape
    source = sources()
    tops, totals, picks = [stats[:, i, :rows] for i in range(3)]
    top = jnp.max(tops, axis=0, keepdims=True)
    logz = top + jnp.log(jnp.sum(totals * jnp.exp(tops - top), axis=0, keepdims=True))
    picked[...] = jnp.sum(picks, axis=0, keepdims=True) - logz
    square = jnp.concatenate(
        [jnp.broadcast_to(logz, (128, rows)), jnp.zeros((128, 128 - rows), F32)], axis=1
    )
    column = square.T[:rows, :1]
    for i in range(pieces):
        at = pl.multiple_of(source[i] * width, width)
        out[:, pl.ds(at, width)] = home[i] - column


def call(kernel, shapes, *args, cost=None):
    outs = [jax.ShapeDtypeStruct(s, d) for s, d in shapes]
    result = pl.pallas_call(
        kernel,
        in_specs=[pl.BlockSpec() for _ in args],
        out_specs=[pl.BlockSpec() for _ in outs],
        out_shape=outs,
        compiler_params=pltpu.CompilerParams(vmem_limit_bytes=16 << 20),
        cost_estimate=cost,
    )(*args)
    return result if len(outs) > 1 else result[0]


def shards(
    base_hidden,
    expert_hidden,
    anti_hidden,
    base_gain,
    expert_gain,
    anti_gain,
    base_head,
    expert_head,
    anti_head,
    strength,
    token_ids,
):
    rows, c_width = token_ids.shape[0], base_head.shape[2]

    quarter = expert_head.shape[0]
    heads = []

    def swap(value, moves, *beside):
        ready = together(value, *[head for head, _ in beside])
        got = [exchange(ready[0], *move) for move in moves]
        done = [relay(h, start, quarter) for h, (_, start) in zip(ready[1:], beside)]
        results = together(*got, *done)
        heads.extend(results[len(moves) :])
        return results[: len(moves)]

    hidden = (base_hidden, expert_hidden, anti_hidden)
    gains = [in_hbm(g) for g in (base_gain, expert_gain, anti_gain)]
    width = sum(h.shape[1] for h in hidden)
    flat = [in_hbm(h) for h in hidden]
    sums = call(square_kernel, [((NY * NX, 8, 128), F32)], *flat)
    sums = lax.all_to_all(sums, "tensor", 0, 0, tiled=True)
    normed = call(
        functools.partial(norm_kernel, (D, DE, DE)),
        [((rows, width), BF)],
        *flat,
        *gains,
        sums,
        cost=LONG,
    )
    strength, normed = together(strength, normed)
    along_z = [("z", 0, k) for k in ALONG_Z]
    got = swap(normed, along_z, (base_head, 0), (base_head, quarter), (expert_head, 0))
    mine = jnp.concatenate([normed, *got])
    (other,) = swap(mine, [("core",)], (anti_head, 0))
    acts = call(join_kernel, [((NZ * NC * rows, width), BF)], mine, other)

    axes = (("x", "y"), ("y", "x"))
    kept = [[], []]
    moved = [[], []]
    second_step = []
    for i in range(4):
        for half in range(2):
            kind = BF if i < 2 else F32
            part = project(strength, acts, heads, i, half, kind)
            acts, part = together(acts, part)
            if i < 2:
                moved[half].append(exchange(part, axes[half][0], 0))
            else:
                kept[half].append(part)
        if i == 2:
            totals = [narrow(kept[h][0] + wide(moved[h][0])) for h in range(2)]
            second_step = [exchange(totals[h], axes[h][0], 1) for h in range(2)]
            acts, _ = together(acts, totals[1])
    own = together(kept[0][1], kept[1][1])
    sums = together(*[own[h] + wide(moved[h][1]) for h in range(2)])
    sums = [sums[h] + wide(second_step[h]) for h in range(2)]
    moved = [
        [exchange(narrow(sums[h][i]), axes[h][1], 0) for i in (1, 0)] for h in range(2)
    ]
    second_step = [
        exchange(narrow(sums[h][3] + wide(moved[h][0])), axes[h][1], 1) for h in range(2)
    ]
    logits = jnp.concatenate(
        [narrow(sums[h][2] + wide(moved[h][1]) + wide(second_step[h])) for h in range(2)], axis=1
    ).reshape(NC, NZ, rows, c_width)

    other = exchange(logits[1], "core")
    home = [jnp.stack([logits[0, 0], other[0]])]
    for k in HOME_Z:
        i = 1 + ALONG_Z.index(k)
        home.append(exchange(jnp.stack([logits[0, i], other[i]]), "z", by=k))
    home = wide(jnp.concatenate(home))

    stats = call(stats_kernel, [((NY * NX, 8, 128), F32)], home, in_hbm(token_ids))
    stats = lax.all_to_all(stats, "tensor", 0, 0, tiled=True)
    log_probs, picked = call(
        final_kernel, [((rows, 8 * c_width), F32), ((1, rows), F32)], home, stats
    )
    return log_probs, picked[0]


def solution(mesh):
    return jax.shard_map(
        shards,
        mesh=mesh,
        in_specs=(
            P("rows", "tensor"),
            P("rows", "tensor"),
            P("rows", "tensor"),
            P("tensor"),
            P("tensor"),
            P("tensor"),
            P("tensor", None, "rows"),
            P("tensor", None, "rows"),
            P("tensor", None, "rows"),
            P(),
            P("rows"),
        ),
        out_specs=(P("rows", "tensor"), P("rows")),
        check_vma=False,
    )
```

```python
import functools

import jax
import jax.numpy as jnp
from jax import lax
from jax.experimental import pallas as pl
from jax.experimental.pallas import tpu as pltpu
from jax.sharding import PartitionSpec as P

D = 8192
DE = 4096
VOCAB = 65536
NZ, NC, NY, NX = 4, 2, 4, 4
AXES = ("rows", "tensor")
BF = jnp.bfloat16
F16 = jnp.float16
F32 = jnp.float32
DOWN, UP = 0.0625, 16.0
LONG = pl.CostEstimate(flops=10**10, bytes_accessed=2**24, transcendentals=0)
ALONG_Z = (1, 3, 2)
HOME_Z = (2, 1, 3)


def device(z, c, y, x):
    return (z * NC + c) * (NY * NX) + y * NX + x


def exchange(value, axis, stage=0, by=None):
    pairs = []
    for z in range(NZ):
        for c in range(NC):
            u = by or (1 if (stage + c) % 2 == 0 else 3)
            for y in range(NY):
                for x in range(NX):
                    to = {
                        "z": (z ^ u, c, y, x),
                        "y": (z, c, y ^ u, x),
                        "x": (z, c, y, x ^ u),
                        "core": (z, 1 - c, y, x),
                    }[axis]
                    pairs.append((device(z, c, y, x), device(*to)))
    return lax.ppermute(value, AXES, pairs)


def here():
    r, t = lax.axis_index("rows"), lax.axis_index("tensor")
    return r // NC, r % NC, t // NX, t % NX


def sources():
    z, c, _, _ = here()
    return [(z ^ k) * NC + core for k in (0,) + HOME_Z for core in (c, 1 - c)]


def relay_kernel(head, out):
    out[...] = jnp.swapaxes(head[...], 0, 1)


def relay(head, start, count, step=64):
    _, n_a, c = head.shape
    return pl.pallas_call(
        relay_kernel,
        grid=(count // step,),
        in_specs=[pl.BlockSpec((step, n_a, c), lambda i: (start // step + i, 0, 0))],
        out_specs=pl.BlockSpec((n_a, step, c), lambda i: (0, i, 0)),
        out_shape=jax.ShapeDtypeStruct((n_a, count, c), head.dtype),
        compiler_params=pltpu.CompilerParams(vmem_limit_bytes=12 << 20),
        cost_estimate=pl.CostEstimate(flops=0, bytes_accessed=2**23, transcendentals=0),
    )(head)


def matmul_kernel(step, half, alpha, acts, wb0, wb1, we, wa, out):
    quarter, cols = wb0.shape[1], out.shape[2]
    _, c, y, x = here()
    u, v = 1 + 2 * c, 3 - 2 * c
    first, second = (2, u, v, 0)[step], (u, 2, 0, v)
    for i in range(out.shape[0]):
        along_y, along_x = (second[i], first) if half == 0 else (first, second[i])
        block = (y ^ along_y) * NX + (x ^ along_x)
        base0, base1, expert, anti = [
            jnp.dot(
                acts[:, j * quarter : (j + 1) * quarter],
                w[block, :, half * cols : (half + 1) * cols],
                preferred_element_type=F32,
            )
            for j, w in enumerate((wb0, wb1, we, wa))
        ]
        total = base0 + base1 + alpha[0] * (expert - anti)
        out[i] = total.astype(out.dtype)


def project(alpha, acts, heads, step, half, dtype):
    smem = pl.BlockSpec(memory_space=pltpu.SMEM)
    vmem = pl.BlockSpec(memory_space=pltpu.VMEM)
    return pl.pallas_call(
        functools.partial(matmul_kernel, step, half),
        in_specs=[smem] + [vmem] * (1 + len(heads)),
        out_specs=vmem,
        out_shape=jax.ShapeDtypeStruct((4, acts.shape[0], heads[0].shape[2] // 2), dtype),
        compiler_params=pltpu.CompilerParams(vmem_limit_bytes=12 << 20),
        cost_estimate=pl.CostEstimate(flops=1, bytes_accessed=1, transcendentals=0),
    )(alpha, acts, *heads)


def wide(value):
    return value.astype(F32) * UP if value.dtype == F16 else value.astype(F32)


def narrow(value):
    return (value * DOWN).astype(F16)


def in_hbm(value):
    return pltpu.with_memory_space_constraint(value, pltpu.HBM)


def together(*values):
    return lax.optimization_barrier(values)


def lanes(columns, rows):
    lane = lax.broadcasted_iota(jnp.int32, (rows, 128), 1)
    out = jnp.zeros((rows, 128), F32)
    for i, column in enumerate(columns):
        out = jnp.where(lane == i, column, out)
    return out


def to_all(out, columns):
    rows = columns[0].shape[0]
    square = jnp.concatenate([lanes(columns, rows), jnp.zeros((128 - rows, 128), F32)])
    out[...] = jnp.broadcast_to(square.T[None, :8], out.shape)


def square_kernel(*refs):
    values = [h[...].astype(F32) for h in refs[:-1]]
    to_all(refs[-1], [jnp.sum(h * h, axis=1, keepdims=True) for h in values])


def norm_kernel(widths, *refs):
    hidden, gains, sums, out = refs[:3], refs[3:6], refs[6], refs[7]
    total = jnp.sum(sums[...], axis=0)
    total = jnp.concatenate([total, jnp.zeros((120, 128), F32)]).T[: out.shape[0]]
    at = 0
    for i, h in enumerate(hidden):
        scale = lax.rsqrt(total[:, i : i + 1] / widths[i] + 1e-05)
        value = h[...].astype(F32) * scale * gains[i][...].astype(F32)[None]
        out[:, at : at + h.shape[1]] = value.astype(out.dtype)
        at += h.shape[1]


def stats_kernel(home, ids, out):
    pieces, rows, width = home.shape
    source = sources()
    row = ids[...][None].astype(F32)
    row = jnp.concatenate([row, jnp.zeros((1, 128 - rows), F32)], axis=1)
    column = jnp.broadcast_to(row, (128, 128)).T[:rows, :1]
    wanted = column.astype(jnp.int32) - lax.axis_index("tensor") * (VOCAB // (NY * NX))
    top = jnp.max(home[...], axis=(0,))
    top = jnp.max(top, axis=1, keepdims=True)
    total = jnp.zeros((rows, width), F32)
    pick = jnp.zeros((rows, width), F32)
    lane = lax.broadcasted_iota(jnp.int32, (rows, width), 1)
    for i in range(pieces):
        value = home[i]
        total += jnp.exp(value - top)
        pick += jnp.where(lane == wanted - source[i] * width, value, 0.0)
    total = jnp.sum(total, axis=1, keepdims=True)
    pick = jnp.sum(pick, axis=1, keepdims=True)
    to_all(out, [top, total, pick])


def final_kernel(home, stats, out, picked):
    pieces, rows, width = home.shape
    source = sources()
    tops, totals, picks = [stats[:, i, :rows] for i in range(3)]
    top = jnp.max(tops, axis=0, keepdims=True)
    logz = top + jnp.log(jnp.sum(totals * jnp.exp(tops - top), axis=0, keepdims=True))
    picked[...] = jnp.sum(picks, axis=0, keepdims=True) - logz
    square = jnp.concatenate(
        [jnp.broadcast_to(logz, (128, rows)), jnp.zeros((128, 128 - rows), F32)], axis=1
    )
    column = square.T[:rows, :1]
    for i in range(pieces):
        at = pl.multiple_of(source[i] * width, width)
        out[:, pl.ds(at, width)] = home[i] - column


def call(kernel, shapes, *args, cost=None):
    outs = [jax.ShapeDtypeStruct(s, d) for s, d in shapes]
    result = pl.pallas_call(
        kernel,
        in_specs=[pl.BlockSpec() for _ in args],
        out_specs=[pl.BlockSpec() for _ in outs],
        out_shape=outs,
        compiler_params=pltpu.CompilerParams(vmem_limit_bytes=16 << 20),
        cost_estimate=cost,
    )(*args)
    return result if len(outs) > 1 else result[0]


def shards(
    base_hidden,
    expert_hidden,
    anti_hidden,
    base_gain,
    expert_gain,
    anti_gain,
    base_head,
    expert_head,
    anti_head,
    strength,
    token_ids,
):
    rows, c_width = token_ids.shape[0], base_head.shape[2]

    quarter = expert_head.shape[0]
    heads = []

    def swap(value, moves, *beside):
        ready = together(value, *[head for head, _ in beside])
        got = [exchange(ready[0], *move) for move in moves]
        done = [relay(h, start, quarter) for h, (_, start) in zip(ready[1:], beside)]
        results = together(*got, *done)
        heads.extend(results[len(moves) :])
        return results[: len(moves)]

    hidden = (base_hidden, expert_hidden, anti_hidden)
    gains = [in_hbm(g) for g in (base_gain, expert_gain, anti_gain)]
    width = sum(h.shape[1] for h in hidden)
    flat = [in_hbm(h) for h in hidden]
    sums = call(square_kernel, [((NY * NX, 8, 128), F32)], *flat)
    sums = lax.all_to_all(sums, "tensor", 0, 0, tiled=True)
    normed = call(
        functools.partial(norm_kernel, (D, DE, DE)),
        [((rows, width), BF)],
        *flat,
        *gains,
        sums,
        cost=LONG,
    )
    strength, normed = together(strength, normed)
    along_z = [("z", 0, k) for k in ALONG_Z]
    got = swap(normed, along_z, (base_head, 0), (base_head, quarter), (expert_head, 0))
    mine = jnp.concatenate([normed, *got])
    (other,) = swap(mine, [("core",)], (anti_head, 0))
    acts = jnp.concatenate([mine, other])

    axes = (("x", "y"), ("y", "x"))
    kept = [[], []]
    moved = [[], []]
    second_step = []
    for i in range(4):
        for half in range(2):
            kind = BF if i < 2 else F32
            part = project(strength, acts, heads, i, half, kind)
            acts, part = together(acts, part)
            if i < 2:
                moved[half].append(exchange(part, axes[half][0], 0))
            else:
                kept[half].append(part)
        if i == 2:
            totals = [narrow(kept[h][0] + wide(moved[h][0])) for h in range(2)]
            second_step = [exchange(totals[h], axes[h][0], 1) for h in range(2)]
            acts, _ = together(acts, totals[1])
    own = together(kept[0][1], kept[1][1])
    sums = together(*[own[h] + wide(moved[h][1]) for h in range(2)])
    sums = [sums[h] + wide(second_step[h]) for h in range(2)]
    moved = [
        [exchange(narrow(sums[h][i]), axes[h][1], 0) for i in (1, 0)] for h in range(2)
    ]
    second_step = [
        exchange(narrow(sums[h][3] + wide(moved[h][0])), axes[h][1], 1) for h in range(2)
    ]
    logits = jnp.concatenate(
        [narrow(sums[h][2] + wide(moved[h][1]) + wide(second_step[h])) for h in range(2)], axis=1
    ).reshape(NC, NZ, rows, c_width)

    other = exchange(logits[1], "core")
    home = [jnp.stack([logits[0, 0], other[0]])]
    for k in HOME_Z:
        i = 1 + ALONG_Z.index(k)
        home.append(exchange(jnp.stack([logits[0, i], other[i]]), "z", by=k))
    home = wide(jnp.concatenate(home))

    stats = call(stats_kernel, [((NY * NX, 8, 128), F32)], home, in_hbm(token_ids))
    stats = lax.all_to_all(stats, "tensor", 0, 0, tiled=True)
    log_probs, picked = call(
        final_kernel, [((rows, 8 * c_width), F32), ((1, rows), F32)], home, stats
    )
    return log_probs, picked[0]


def solution(mesh):
    return jax.shard_map(
        shards,
        mesh=mesh,
        in_specs=(
            P("rows", "tensor"),
            P("rows", "tensor"),
            P("rows", "tensor"),
            P("tensor"),
            P("tensor"),
            P("tensor"),
            P("tensor", None, "rows"),
            P("tensor", None, "rows"),
            P("tensor", None, "rows"),
            P(),
            P("rows"),
        ),
        out_specs=(P("rows", "tensor"), P("rows")),
        check_vma=False,
    )
```
